32 devices in a mesh: dp: 8 (over y, x, core), tensor: 4 (over z).
Axes of the slice: x: 2, y: 2, z: 4, core: 2. Of those that a mesh axis runs over, the one named last changes fastest.
Arguments:
- block_input: bfloat16 [8, 512, 768], P('dp', 'tensor'), may hold values from -6 to 6
- segment_ids: int32 [8, 512], P('dp', 'tensor'), may hold values from 0 to 3, never falling along the last dimension, each value on 1 to 256 neighbouring positions
- w_qkv: bfloat16 [3, 768, 768], P(None, 'dp', 'tensor'), may hold values from -2.16506351 to 2.16506351
- w_out: bfloat16 [768, 768], P('tensor', 'dp'), may hold values from -0.875 to 0.875
- w_in: bfloat16 [768, 3072], P('dp', 'tensor'), may hold values from -0.21875 to 0.21875
- w_back: bfloat16 [3072, 768], P('tensor', 'dp'), may hold values from -0.21875 to 0.21875
- qv_bias: float32 [2, 768], P(None, 'tensor'), may hold values from -3 to 3
- in_bias: float32 [3072], P('tensor'), may hold values from -3 to 3
- norm_gains: float32 [2, 768], replicated, may hold values from 0.5 to 1.5
- norm_biases: float32 [4, 768], replicated, may hold values from -2 to 2
- out_cotangent: bfloat16 [8, 512, 768], P('dp', 'tensor'), may hold values from -6 to 6
Outputs:
- block_output: bfloat16 [8, 512, 768], P('dp', 'tensor')
- input_grad: float32 [8, 512, 768], P('dp', 'tensor')
- grad_qkv: float32 [3, 768, 768], P(None, 'dp', 'tensor')
- grad_out: float32 [768, 768], P('tensor', 'dp')
- grad_in: float32 [768, 3072], P('dp', 'tensor')
- grad_back: float32 [3072, 768], P('tensor', 'dp')
- grad_qv_bias: float32 [2, 768], P(None, 'tensor')
- grad_in_bias: float32 [3072], P('tensor')
- grad_gains: float32 [2, 768], replicated
- grad_biases: float32 [4, 768], replicated
The draws below stay inside these ranges and needn't reach their ends.
Inputs may be any that keep to these rules, and one draw needn't show every extreme that they name: `segment_ids`: within each sequence segment numbers never fall; a document spans at most half of 512 tokens, and one document in each sequence spans exactly that many.
All inputs are finite; a program needn't handle non-finite values.
Results may differ from the reference program's by a relative error of at most 0.0098.
Values may be sent and summed in bfloat16 or wider, within the bound.
A program may use at most 64 MiB of HBM per device.

```python
import math
import jax
import jax.numpy as jnp
import numpy as np
from jax import lax

D = 768
HEADS = 12
FF = 3072
SEQ = 512
DOCS = 4
SEQS = 8


def draw_w_qkv(key, part):
    base_key = jax.random.fold_in(key, 0)
    base = jnp.clip(jax.random.normal(base_key, (3, D, D), jnp.float32), -6.0, 6.0) / math.sqrt(D)
    return base.astype(jnp.bfloat16)


def level_of(own_key, extent, pieces, low, high):
    level = 1.0
    for axis_at, shards_of in pieces:
        heights = jax.random.uniform(jax.random.fold_in(jax.random.fold_in(own_key, 6), axis_at), (shards_of,), jnp.float32, low / len(pieces), high / len(pieces))
        level = level * jnp.repeat(jnp.exp(heights), extent[axis_at] // shards_of).reshape((-1,) + (1,) * (len(extent) - 1 - axis_at))
    return level


def profile(amount, total, bound, lean):
    portions = [(1 << 20) // math.isqrt(rank ** lean) + 1 for rank in range(2, amount + 1)]
    rest, counts = total - bound - (amount - 1), [1] * (amount - 1)
    while rest > 0:
        movable = [i for i in range(amount - 1) if counts[i] < bound]
        mass, left = sum([portions[i] for i in movable]), rest
        for i in movable:
            addition = min(bound - counts[i], max(1, left * portions[i] // mass), rest)
            counts[i] = counts[i] + addition
            rest = rest - addition
    return np.array([bound] + counts)


def uneven_parts(stream_key, count, total, limit, slope):
    if count == 2:
        one = jax.random.randint(stream_key, (), max(1, total - limit), min(limit, total - 1) + 1)
        return jnp.stack([one, total - one])
    lengths = jnp.asarray(profile(count, total, limit, slope), jnp.int32)
    twos = (count - 1) // 2
    giver, taker = lengths[1:1 + 2 * twos:2], lengths[2:2 + 2 * twos:2]
    room = jnp.minimum(giver - 1, limit - taker)
    moved = jax.random.randint(jax.random.fold_in(stream_key, 1), (twos,), 0, 1 << 20) % (room + 1)
    lengths = lengths.at[1:1 + 2 * twos:2].set(giver - moved).at[2:2 + 2 * twos:2].set(taker + moved)
    return lengths[jax.random.permutation(jax.random.fold_in(stream_key, 2), count)]


def bell_draw(key, shape, deviation, reach, pieces=(), kind=jnp.bfloat16):
    entries = deviation * jax.random.normal(key, shape, jnp.float32)
    if pieces:
        entries = entries * level_of(key, shape, pieces, -0.22, 0.18)
    return jnp.clip(entries, -reach, reach).astype(kind)


def setup_inputs(seed: int = 0) -> dict:
    streams_of = jax.random.split(jax.random.key(seed), 12)
    return {
        "block_input": bell_draw(streams_of[0], (SEQS, SEQ, D), 1.0, 6.0, ((0, 8), (1, 4))),
        "segment_ids": jax.vmap(lambda own: jnp.searchsorted(jnp.cumsum(uneven_parts(own, DOCS, SEQ, SEQ // 2, 1)), jnp.arange(SEQ), side="right"))(jax.random.split(streams_of[1], SEQS)).reshape((SEQS, SEQ)).astype(jnp.int32),
        "w_qkv": draw_w_qkv(jax.random.fold_in(streams_of[11], 71), 0),
        "w_out": bell_draw(streams_of[3], (D, D), (D // 16) ** -0.5, 0.875, ((0, 4), (1, 8))),
        "w_in": bell_draw(streams_of[4], (D, FF), D ** -0.5, 0.21875, ((0, 8), (1, 4))),
        "w_back": bell_draw(streams_of[5], (FF, D), (FF // 4) ** -0.5, 0.21875, ((0, 4), (1, 8))),
        "qv_bias": bell_draw(streams_of[6], (2, D), 0.5, 3.0, ((1, 4),), jnp.float32),
        "in_bias": bell_draw(streams_of[7], (FF,), 0.5, 3.0, ((0, 4),), jnp.float32),
        "norm_gains": jnp.clip(jax.random.uniform(streams_of[8], (2, D), jnp.float32, 0.5, 1.5), 0.5, 1.5),
        "norm_biases": bell_draw(streams_of[9], (4, D), 0.3, 2.0, (), jnp.float32),
        "out_cotangent": bell_draw(streams_of[10], (SEQS, SEQ, D), 1.0, 6.0, ((0, 8), (1, 4))),
    }


EPS = 1e-05
GELU_C = math.sqrt(2.0 / math.pi)
GELU_A = 0.044715

def normalize(residual, gain_row, offset_row):
    centered = residual - lax.optimization_barrier(jnp.mean(residual, axis=-1, keepdims=True))
    inv_std = lax.rsqrt(lax.optimization_barrier(jnp.mean(centered * centered, axis=-1, keepdims=True)) + EPS)
    normed = centered * inv_std
    return (normed * gain_row + offset_row, normed, inv_std)

def normalize_back(upstream, normed, inv_std, gain_row):
    scaled = upstream * gain_row
    return inv_std * (scaled - lax.optimization_barrier(jnp.mean(scaled, axis=-1, keepdims=True)) - normed * lax.optimization_barrier(jnp.mean(scaled * normed, axis=-1, keepdims=True)))

def gelu_pair(inputs):
    inner_arg = GELU_C * (inputs + GELU_A * inputs * inputs * inputs)
    tangent_h = jnp.tanh(inner_arg)
    value_out = 0.5 * inputs * (1.0 + tangent_h)
    slope_out = 0.5 * (1.0 + tangent_h) + 0.5 * inputs * (1.0 - tangent_h * tangent_h) * GELU_C * (1.0 + 3.0 * GELU_A * inputs * inputs)
    return (value_out, slope_out)

def masked_scores(query_block, key_rows, segment, row_start, key_end, num_heads):
    block_rows = query_block.shape[0]
    width = query_block.shape[1] // num_heads
    query_heads = query_block.reshape(block_rows, num_heads, width).astype(jnp.float32)
    key_heads = key_rows[:key_end].reshape(key_end, num_heads, width).astype(jnp.float32)
    raw_scores = jnp.einsum('qhd,khd->hqk', query_heads, key_heads) * (1.0 / math.sqrt(width))
    query_pos = row_start + jnp.arange(block_rows, dtype=jnp.int32)
    key_pos = jnp.arange(key_end, dtype=jnp.int32)
    allowed = (key_pos[None, :] <= query_pos[:, None]) & (segment[:key_end][None, :] == segment[row_start:key_end][:, None])
    return jnp.where(allowed[None], raw_scores, -jnp.inf)

def attend_forward(queries, key_rows, values, segment, num_heads):
    total_rows = queries.shape[0]
    block_rows = min(512, total_rows)
    width = queries.shape[1] // num_heads
    contexts = []
    totals = []
    for block_index in range(total_rows // block_rows):
        row_start = block_index * block_rows
        key_end = row_start + block_rows
        scores = masked_scores(queries[row_start:key_end], key_rows, segment, row_start, key_end, num_heads)
        row_max = lax.optimization_barrier(jnp.max(scores, axis=-1, keepdims=True))
        log_total = row_max + jnp.log(lax.optimization_barrier(jnp.sum(jnp.exp(scores - row_max), axis=-1, keepdims=True)))
        weights = jnp.exp(scores - log_total).astype(jnp.bfloat16)
        value_heads = values[:key_end].reshape(key_end, num_heads, width)
        context = jnp.einsum('hqk,khd->qhd', weights.astype(jnp.float32), value_heads.astype(jnp.float32))
        contexts.append(context.reshape(block_rows, num_heads * width).astype(jnp.bfloat16))
        totals.append(log_total)
    return (jnp.concatenate(contexts, axis=0), jnp.concatenate(totals, axis=1))

def attend_backward(queries, key_rows, values, segment, context, log_total, context_grad, num_heads):
    total_rows = queries.shape[0]
    block_rows = min(512, total_rows)
    width = queries.shape[1] // num_heads
    inv_root = 1.0 / math.sqrt(width)
    query_grads = []
    key_grad = jnp.zeros((total_rows, num_heads, width), jnp.float32)
    value_grad = jnp.zeros((total_rows, num_heads, width), jnp.float32)
    for block_index in range(total_rows // block_rows):
        row_start = block_index * block_rows
        key_end = row_start + block_rows
        scores = masked_scores(queries[row_start:key_end], key_rows, segment, row_start, key_end, num_heads)
        probs = jnp.exp(scores - log_total[:, row_start:key_end])
        probs_half = probs.astype(jnp.bfloat16)
        grad_heads = context_grad[row_start:key_end].reshape(block_rows, num_heads, width).astype(jnp.float32)
        context_heads = context[row_start:key_end].reshape(block_rows, num_heads, width).astype(jnp.float32)
        value_heads = values[:key_end].reshape(key_end, num_heads, width).astype(jnp.float32)
        key_heads = key_rows[:key_end].reshape(key_end, num_heads, width).astype(jnp.float32)
        query_heads = queries[row_start:key_end].reshape(block_rows, num_heads, width).astype(jnp.float32)
        prob_grad = jnp.einsum('qhd,khd->hqk', grad_heads, value_heads)
        row_dot = jnp.transpose(lax.optimization_barrier(jnp.sum(grad_heads * context_heads, axis=-1)))[:, :, None]
        score_grad = (probs * (prob_grad - row_dot) * inv_root).astype(jnp.bfloat16).astype(jnp.float32)
        query_grads.append(jnp.einsum('hqk,khd->qhd', score_grad, key_heads).reshape(block_rows, num_heads * width))
        key_grad = key_grad.at[:key_end].add(jnp.einsum('hqk,qhd->khd', score_grad, query_heads))
        value_grad = value_grad.at[:key_end].add(jnp.einsum('hqk,qhd->khd', probs_half.astype(jnp.float32), grad_heads))
    return (jnp.concatenate(query_grads, axis=0), key_grad.reshape(total_rows, num_heads * width), value_grad.reshape(total_rows, num_heads * width))

def reference(block_input, segment_ids, w_qkv, w_out, w_in, w_back, qv_bias, in_bias, norm_gains, norm_biases, out_cotangent):

    def one_sequence(totals, sequence_item):
        inputs, segment, cotangent_half = sequence_item
        residual = inputs.astype(jnp.float32)
        first_out, normed_first, inv_first = normalize(residual, norm_gains[0], norm_biases[0])
        first_half = first_out.astype(jnp.bfloat16)
        projected = jnp.einsum('sd,cde->sce', first_half.astype(jnp.float32), w_qkv.astype(jnp.float32))
        queries = (projected[:, 0] + qv_bias[0]).astype(jnp.bfloat16)
        key_rows = projected[:, 1].astype(jnp.bfloat16)
        values = (projected[:, 2] + qv_bias[1]).astype(jnp.bfloat16)
        context, log_total = attend_forward(queries, key_rows, values, segment, HEADS)
        middle = residual + jnp.dot(context, w_out, preferred_element_type=jnp.float32) + norm_biases[2]
        second_out, normed_second, inv_second = normalize(middle, norm_gains[1], norm_biases[1])
        second_half = second_out.astype(jnp.bfloat16)
        hidden_pre = jnp.dot(second_half, w_in, preferred_element_type=jnp.float32) + in_bias
        gelu_value, gelu_slope = gelu_pair(hidden_pre)
        activation = gelu_value.astype(jnp.bfloat16)
        output_full = middle + jnp.dot(activation, w_back, preferred_element_type=jnp.float32) + norm_biases[3]
        block_out = output_full.astype(jnp.bfloat16)
        cotangent = cotangent_half.astype(jnp.float32)
        grad_back_part = jnp.dot(activation.T, cotangent_half, preferred_element_type=jnp.float32)
        hidden_grad = jnp.dot(cotangent_half, w_back.T, preferred_element_type=jnp.float32) * gelu_slope
        hidden_half = hidden_grad.astype(jnp.bfloat16)
        grad_in_part = jnp.dot(second_half.T, hidden_half, preferred_element_type=jnp.float32)
        second_grad = jnp.dot(hidden_half, w_in.T, preferred_element_type=jnp.float32)
        middle_grad = cotangent + normalize_back(second_grad, normed_second, inv_second, norm_gains[1])
        middle_half = middle_grad.astype(jnp.bfloat16)
        grad_out_part = jnp.dot(context.T, middle_half, preferred_element_type=jnp.float32)
        context_grad = jnp.dot(middle_half, w_out.T, preferred_element_type=jnp.float32).astype(jnp.bfloat16)
        query_grad, key_grad, value_grad = attend_backward(queries, key_rows, values, segment, context, log_total, context_grad, HEADS)
        proj_half = jnp.stack([query_grad, key_grad, value_grad], axis=1).astype(jnp.bfloat16).astype(jnp.float32)
        grad_qkv_part = jnp.einsum('sd,sce->cde', first_half.astype(jnp.float32), proj_half)
        first_grad = jnp.einsum('sce,cde->sd', proj_half, w_qkv.astype(jnp.float32))
        input_grad = middle_grad + normalize_back(first_grad, normed_first, inv_first, norm_gains[0])
        parts = (grad_qkv_part, grad_out_part, grad_in_part, grad_back_part, jnp.stack([lax.optimization_barrier(jnp.sum(query_grad, axis=0)), lax.optimization_barrier(jnp.sum(value_grad, axis=0))]), lax.optimization_barrier(jnp.sum(hidden_grad, axis=0)), jnp.stack([lax.optimization_barrier(jnp.sum(first_grad * normed_first, axis=0)), lax.optimization_barrier(jnp.sum(second_grad * normed_second, axis=0))]), jnp.stack([lax.optimization_barrier(jnp.sum(first_grad, axis=0)), lax.optimization_barrier(jnp.sum(second_grad, axis=0)), lax.optimization_barrier(jnp.sum(middle_grad, axis=0)), lax.optimization_barrier(jnp.sum(cotangent, axis=0))]))
        new_totals = tuple((total + part for total, part in zip(totals, parts)))
        return (new_totals, (block_out, input_grad))
    initial = (jnp.zeros((3, D, D), jnp.float32), jnp.zeros((D, D), jnp.float32), jnp.zeros((D, FF), jnp.float32), jnp.zeros((FF, D), jnp.float32), jnp.zeros((2, D), jnp.float32), jnp.zeros((FF,), jnp.float32), jnp.zeros((2, D), jnp.float32), jnp.zeros((4, D), jnp.float32))
    totals, (outputs, grads) = lax.scan(one_sequence, initial, (block_input, segment_ids, out_cotangent))
    return (outputs, grads, totals[0], totals[1], totals[2], totals[3], totals[4], totals[5], totals[6], totals[7])
```

```python
import math

import jax
import jax.numpy as jnp
from jax import lax
from jax.sharding import PartitionSpec as P

HEAD = 64


EPS = 1e-05
GELU_C = math.sqrt(2.0 / math.pi)
GELU_A = 0.044715


def normalize(residual, gain_row, offset_row):
    centered = residual - jnp.mean(residual, axis=-1, keepdims=True)
    inv_std = lax.rsqrt(jnp.mean(centered * centered, axis=-1, keepdims=True) + EPS)
    normed = centered * inv_std
    return (normed * gain_row + offset_row, normed, inv_std)


def normalize_back(upstream, normed, inv_std, gain_row):
    scaled = upstream * gain_row
    return inv_std * (
        scaled
        - jnp.mean(scaled, axis=-1, keepdims=True)
        - normed * jnp.mean(scaled * normed, axis=-1, keepdims=True)
    )


def gelu_pair(inputs):
    inner_arg = GELU_C * (inputs + GELU_A * inputs * inputs * inputs)
    tangent_h = jnp.tanh(inner_arg)
    value_out = 0.5 * inputs * (1.0 + tangent_h)
    slope_out = 0.5 * (1.0 + tangent_h) + 0.5 * inputs * (1.0 - tangent_h * tangent_h) * GELU_C * (
        1.0 + 3.0 * GELU_A * inputs * inputs
    )
    return (value_out, slope_out)


def contract_rows(left, right):
    return lax.dot_general(
        left, right, (((0,), (0,)), ((), ())), preferred_element_type=jnp.float32
    )


def contract_cols(left, right):
    return lax.dot_general(
        left, right, (((1,), (1,)), ((), ())), preferred_element_type=jnp.float32
    )


def masked_scores(query_block, key_rows, segment, key_end, num_heads):
    block_rows = query_block.shape[0]
    width = query_block.shape[1] // num_heads
    query_heads = query_block.reshape(block_rows, num_heads, width)
    key_heads = key_rows.reshape(key_end, num_heads, width)
    raw_scores = jnp.einsum(
        "qhd,khd->hqk", query_heads, key_heads, preferred_element_type=jnp.float32
    ) * (1.0 / math.sqrt(width))
    query_pos = jnp.arange(block_rows, dtype=jnp.int32)
    key_pos = jnp.arange(key_end, dtype=jnp.int32)
    allowed = (key_pos[None, :] <= query_pos[:, None]) & (segment[None, :] == segment[:, None])
    return jnp.where(allowed[None], raw_scores, -jnp.inf)


def attend_forward(queries, key_rows, values, segment, num_heads):
    total_rows = queries.shape[0]
    block_rows = min(512, total_rows)
    width = queries.shape[1] // num_heads
    scores = masked_scores(queries, key_rows, segment, block_rows, num_heads)
    row_max = jnp.max(scores, axis=-1, keepdims=True)
    log_total = row_max + jnp.log(jnp.sum(jnp.exp(scores - row_max), axis=-1, keepdims=True))
    weights = jnp.exp(scores - log_total).astype(jnp.bfloat16)
    value_heads = values.reshape(block_rows, num_heads, width)
    context = jnp.einsum("hqk,khd->qhd", weights, value_heads, preferred_element_type=jnp.float32)
    contexts = context.reshape(block_rows, num_heads * width).astype(jnp.bfloat16)
    return (contexts, log_total)


def attend_backward(
    queries, key_rows, values, segment, context, log_total, context_grad, num_heads
):
    total_rows = queries.shape[0]
    block_rows = min(512, total_rows)
    width = queries.shape[1] // num_heads
    inv_root = 1.0 / math.sqrt(width)
    key_grad = jnp.zeros((total_rows, num_heads, width), jnp.float32)
    value_grad = jnp.zeros((total_rows, num_heads, width), jnp.float32)
    scores = masked_scores(queries, key_rows, segment, block_rows, num_heads)
    probs = jnp.exp(scores - log_total)
    probs_half = probs.astype(jnp.bfloat16)
    grad_heads = context_grad.reshape(block_rows, num_heads, width)
    context_heads = context.reshape(block_rows, num_heads, width)
    value_heads = values.reshape(block_rows, num_heads, width)
    key_heads = key_rows.reshape(block_rows, num_heads, width)
    query_heads = queries.reshape(block_rows, num_heads, width)
    prob_grad = jnp.einsum(
        "qhd,khd->hqk", grad_heads, value_heads, preferred_element_type=jnp.float32
    )
    row_dot = jnp.transpose(
        jnp.sum(grad_heads.astype(jnp.float32) * context_heads.astype(jnp.float32), axis=-1)
    )[:, :, None]
    score_grad = (probs * (prob_grad - row_dot) * inv_root).astype(jnp.bfloat16)
    query_grads = jnp.einsum(
        "hqk,khd->qhd", score_grad, key_heads, preferred_element_type=jnp.float32
    ).reshape(block_rows, num_heads * width)
    key_grad = key_grad.at[:block_rows].add(
        jnp.einsum("hqk,qhd->khd", score_grad, query_heads, preferred_element_type=jnp.float32)
    )
    value_grad = value_grad.at[:block_rows].add(
        jnp.einsum("hqk,qhd->khd", probs_half, grad_heads, preferred_element_type=jnp.float32)
    )
    return (
        query_grads,
        key_grad.reshape(total_rows, num_heads * width),
        value_grad.reshape(total_rows, num_heads * width),
    )


def half_scatter(share):
    return lax.psum_scatter(
        share.astype(jnp.bfloat16), "tensor", scatter_dimension=0, tiled=True
    ).astype(jnp.float32)


def shards(
    block_input,
    segment_ids,
    w_qkv,
    w_out,
    w_in,
    w_back,
    qv_bias,
    in_bias,
    norm_gains,
    norm_biases,
    out_cotangent,
):
    bf16 = jnp.bfloat16
    residual = block_input[0].astype(jnp.float32)
    head_cols = w_qkv.shape[2]
    hidden_cols = w_in.shape[1]
    local_heads = head_cols // HEAD
    cuts = [head_cols, 2 * head_cols, 3 * head_cols, 4 * head_cols, 4 * head_cols + hidden_cols]
    packed = jnp.concatenate([w_qkv[0], w_qkv[1], w_qkv[2], w_out.T, w_in, w_back.T], axis=1)
    full = lax.all_gather(packed, "dp", axis=0, tiled=True)
    qkv_full = full[:, : cuts[2]]
    out_full = full[:, cuts[2] : cuts[3]]
    in_full = full[:, cuts[3] : cuts[4]]
    back_full = full[:, cuts[4] :]
    first_out, normed_first, inv_first = normalize(residual, norm_gains[0], norm_biases[0])
    first_half, segment, cotangent_full = (
        lax.all_gather(first_out.astype(bf16), "tensor", axis=0, tiled=True),
        lax.all_gather(segment_ids[0], "tensor", axis=0, tiled=True),
        lax.all_gather(out_cotangent[0], "tensor", axis=0, tiled=True),
    )
    projected = jnp.dot(first_half, qkv_full, preferred_element_type=jnp.float32)
    queries = (projected[:, : cuts[0]] + qv_bias[0]).astype(bf16)
    key_rows = projected[:, cuts[0] : cuts[1]].astype(bf16)
    values = (projected[:, cuts[1] :] + qv_bias[1]).astype(bf16)
    context, log_total = attend_forward(queries, key_rows, values, segment, local_heads)
    attn_share = half_scatter(contract_cols(context, out_full))
    middle = residual + attn_share + norm_biases[2]
    second_out, normed_second, inv_second = normalize(middle, norm_gains[1], norm_biases[1])
    second_half = lax.all_gather(second_out.astype(bf16), "tensor", axis=0, tiled=True)
    hidden_pre = jnp.dot(second_half, in_full, preferred_element_type=jnp.float32) + in_bias
    gelu_value, gelu_slope = gelu_pair(hidden_pre)
    activation = gelu_value.astype(bf16)
    mlp_share = half_scatter(contract_cols(activation, back_full))
    block_out = (middle + mlp_share + norm_biases[3]).astype(bf16)
    cotangent = out_cotangent[0].astype(jnp.float32)
    grad_back_part = contract_rows(cotangent_full, activation)
    hidden_grad = jnp.dot(cotangent_full, back_full, preferred_element_type=jnp.float32) * gelu_slope
    hidden_half = hidden_grad.astype(bf16)
    grad_in_part = contract_rows(second_half, hidden_half)
    second_grad = half_scatter(contract_cols(hidden_half, in_full))
    middle_grad = cotangent + normalize_back(second_grad, normed_second, inv_second, norm_gains[1])
    middle_full = lax.all_gather(middle_grad.astype(bf16), "tensor", axis=0, tiled=True)
    grad_out_part = contract_rows(middle_full, context)
    context_grad = jnp.dot(middle_full, out_full, preferred_element_type=jnp.float32).astype(bf16)
    query_grad, key_grad, value_grad = attend_backward(
        queries, key_rows, values, segment, context, log_total, context_grad, local_heads
    )
    proj_half = jnp.concatenate([query_grad, key_grad, value_grad], axis=1).astype(bf16)
    grad_qkv_part = contract_rows(first_half, proj_half)
    first_grad = half_scatter(contract_cols(proj_half, qkv_full))
    input_grad = middle_grad + normalize_back(first_grad, normed_first, inv_first, norm_gains[0])
    parts = jnp.concatenate(
        [grad_qkv_part, grad_out_part, grad_in_part, grad_back_part], axis=1
    ).astype(bf16)
    grads = lax.psum_scatter(parts, "dp", scatter_dimension=0, tiled=True).astype(jnp.float32)
    grad_qkv = jnp.stack([grads[:, : cuts[0]], grads[:, cuts[0] : cuts[1]], grads[:, cuts[1] : cuts[2]]])
    grad_out = grads[:, cuts[2] : cuts[3]].T
    grad_in = grads[:, cuts[3] : cuts[4]]
    grad_back = grads[:, cuts[4] :].T
    own = jnp.concatenate(
        [jnp.sum(query_grad, axis=0), jnp.sum(value_grad, axis=0), jnp.sum(hidden_grad, axis=0)]
    )
    tensors = lax.axis_size("tensor")
    rank = lax.axis_index("tensor")
    spread = jnp.where(jnp.arange(tensors)[:, None] == rank, own[None], 0.0)
    norm_terms = jnp.stack(
        [
            jnp.sum(first_grad * normed_first, axis=0),
            jnp.sum(second_grad * normed_second, axis=0),
            jnp.sum(first_grad, axis=0),
            jnp.sum(second_grad, axis=0),
            jnp.sum(middle_grad, axis=0),
            jnp.sum(cotangent, axis=0),
        ]
    )
    total = lax.psum(
        jnp.concatenate([spread.reshape(-1), norm_terms.reshape(-1)]), ("dp", "tensor")
    )
    width = own.shape[0]
    own_total = lax.dynamic_slice(total, (rank * width,), (width,))
    norm_total = total[tensors * width :].reshape(norm_terms.shape)
    return (
        block_out[None],
        input_grad[None],
        grad_qkv,
        grad_out,
        grad_in,
        grad_back,
        own_total[: 2 * head_cols].reshape(2, head_cols),
        own_total[2 * head_cols :],
        norm_total[:2],
        norm_total[2:],
    )


def solution(mesh):
    in_specs = (
        P("dp", "tensor", None),
        P("dp", "tensor"),
        P(None, "dp", "tensor"),
        P("tensor", "dp"),
        P("dp", "tensor"),
        P("tensor", "dp"),
        P(None, "tensor"),
        P("tensor"),
        P(),
        P(),
        P("dp", "tensor", None),
    )
    out_specs = (
        P("dp", "tensor", None),
        P("dp", "tensor", None),
        P(None, "dp", "tensor"),
        P("tensor", "dp"),
        P("dp", "tensor"),
        P("tensor", "dp"),
        P(None, "tensor"),
        P("tensor"),
        P(),
        P(),
    )
    return jax.shard_map(shards, mesh=mesh, in_specs=in_specs, out_specs=out_specs, check_vma=False)
```

```python
import functools
import math

import jax
import jax.numpy as jnp
from jax import lax
from jax.experimental import pallas as pl
from jax.experimental.pallas import tpu as pltpu
from jax.sharding import PartitionSpec as P

HEAD = 64


EPS = 1e-05
GELU_C = math.sqrt(2.0 / math.pi)
GELU_A = 0.044715


def normalize(residual, gain_row, offset_row):
    centered = residual - jnp.mean(residual, axis=-1, keepdims=True)
    inv_std = lax.rsqrt(jnp.mean(centered * centered, axis=-1, keepdims=True) + EPS)
    normed = centered * inv_std
    return (normed * gain_row + offset_row, normed, inv_std)


def normalize_back(upstream, normed, inv_std, gain_row):
    scaled = upstream * gain_row
    return inv_std * (
        scaled
        - jnp.mean(scaled, axis=-1, keepdims=True)
        - normed * jnp.mean(scaled * normed, axis=-1, keepdims=True)
    )


def gelu_pair(inputs):
    inner_arg = GELU_C * (inputs + GELU_A * inputs * inputs * inputs)
    tangent_h = jnp.tanh(inner_arg)
    value_out = 0.5 * inputs * (1.0 + tangent_h)
    slope_out = 0.5 * (1.0 + tangent_h) + 0.5 * inputs * (1.0 - tangent_h * tangent_h) * GELU_C * (
        1.0 + 3.0 * GELU_A * inputs * inputs
    )
    return (value_out, slope_out)


def contract_rows(left, right):
    return lax.dot_general(
        left, right, (((0,), (0,)), ((), ())), preferred_element_type=jnp.float32
    )


def contract_cols(left, right):
    return lax.dot_general(
        left, right, (((1,), (1,)), ((), ())), preferred_element_type=jnp.float32
    )


def masked_scores(query_block, key_rows, segment, key_end, num_heads):
    block_rows = query_block.shape[0]
    width = query_block.shape[1] // num_heads
    query_heads = query_block.reshape(block_rows, num_heads, width)
    key_heads = key_rows.reshape(key_end, num_heads, width)
    raw_scores = jnp.einsum(
        "qhd,khd->hqk", query_heads, key_heads, preferred_element_type=jnp.float32
    ) * (1.0 / math.sqrt(width))
    query_pos = jnp.arange(block_rows, dtype=jnp.int32)
    key_pos = jnp.arange(key_end, dtype=jnp.int32)
    allowed = (key_pos[None, :] <= query_pos[:, None]) & (segment[None, :] == segment[:, None])
    return jnp.where(allowed[None], raw_scores, -jnp.inf)


def attend_forward(queries, key_rows, values, segment, num_heads):
    total_rows = queries.shape[0]
    block_rows = min(512, total_rows)
    width = queries.shape[1] // num_heads
    scores = masked_scores(queries, key_rows, segment, block_rows, num_heads)
    row_max = jnp.max(scores, axis=-1, keepdims=True)
    log_total = row_max + jnp.log(jnp.sum(jnp.exp(scores - row_max), axis=-1, keepdims=True))
    weights = jnp.exp(scores - log_total).astype(jnp.bfloat16)
    value_heads = values.reshape(block_rows, num_heads, width)
    context = jnp.einsum("hqk,khd->qhd", weights, value_heads, preferred_element_type=jnp.float32)
    contexts = context.reshape(block_rows, num_heads * width).astype(jnp.bfloat16)
    return (contexts, log_total)


def attend_backward(
    queries, key_rows, values, segment, context, log_total, context_grad, num_heads
):
    total_rows = queries.shape[0]
    block_rows = min(512, total_rows)
    width = queries.shape[1] // num_heads
    inv_root = 1.0 / math.sqrt(width)
    key_grad = jnp.zeros((total_rows, num_heads, width), jnp.float32)
    value_grad = jnp.zeros((total_rows, num_heads, width), jnp.float32)
    scores = masked_scores(queries, key_rows, segment, block_rows, num_heads)
    probs = jnp.exp(scores - log_total)
    probs_half = probs.astype(jnp.bfloat16)
    grad_heads = context_grad.reshape(block_rows, num_heads, width)
    context_heads = context.reshape(block_rows, num_heads, width)
    value_heads = values.reshape(block_rows, num_heads, width)
    key_heads = key_rows.reshape(block_rows, num_heads, width)
    query_heads = queries.reshape(block_rows, num_heads, width)
    prob_grad = jnp.einsum(
        "qhd,khd->hqk", grad_heads, value_heads, preferred_element_type=jnp.float32
    )
    row_dot = jnp.transpose(
        jnp.sum(grad_heads.astype(jnp.float32) * context_heads.astype(jnp.float32), axis=-1)
    )[:, :, None]
    score_grad = (probs * (prob_grad - row_dot) * inv_root).astype(jnp.bfloat16)
    query_grads = jnp.einsum(
        "hqk,khd->qhd", score_grad, key_heads, preferred_element_type=jnp.float32
    ).reshape(block_rows, num_heads * width)
    key_grad = key_grad.at[:block_rows].add(
        jnp.einsum("hqk,qhd->khd", score_grad, query_heads, preferred_element_type=jnp.float32)
    )
    value_grad = value_grad.at[:block_rows].add(
        jnp.einsum("hqk,qhd->khd", probs_half, grad_heads, preferred_element_type=jnp.float32)
    )
    return (
        query_grads,
        key_grad.reshape(total_rows, num_heads * width),
        value_grad.reshape(total_rows, num_heads * width),
    )


def half_scatter(share):
    return lax.psum_scatter(
        share.astype(jnp.bfloat16), "tensor", scatter_dimension=0, tiled=True
    ).astype(jnp.float32)


def shards(
    block_input,
    segment_ids,
    w_qkv,
    w_out,
    w_in,
    w_back,
    qv_bias,
    in_bias,
    norm_gains,
    norm_biases,
    out_cotangent,
):
    bf16 = jnp.bfloat16
    residual = block_input[0].astype(jnp.float32)
    head_cols = w_qkv.shape[2]
    hidden_cols = w_in.shape[1]
    local_heads = head_cols // HEAD
    cuts = [head_cols, 2 * head_cols, 3 * head_cols, 4 * head_cols, 4 * head_cols + hidden_cols]
    packed = jnp.concatenate([w_qkv[0], w_qkv[1], w_qkv[2], w_out.T, w_in, w_back.T], axis=1)
    full = lax.all_gather(packed, "dp", axis=0, tiled=True)
    qkv_full = full[:, : cuts[2]]
    out_full = full[:, cuts[2] : cuts[3]]
    in_full = full[:, cuts[3] : cuts[4]]
    back_full = full[:, cuts[4] :]
    first_out, normed_first, inv_first = normalize(residual, norm_gains[0], norm_biases[0])
    first_half, segment, cotangent_full = (
        lax.all_gather(first_out.astype(bf16), "tensor", axis=0, tiled=True),
        lax.all_gather(segment_ids[0], "tensor", axis=0, tiled=True),
        lax.all_gather(out_cotangent[0], "tensor", axis=0, tiled=True),
    )
    projected = jnp.dot(first_half, qkv_full, preferred_element_type=jnp.float32)
    queries = (projected[:, : cuts[0]] + qv_bias[0]).astype(bf16)
    key_rows = projected[:, cuts[0] : cuts[1]].astype(bf16)
    values = (projected[:, cuts[1] :] + qv_bias[1]).astype(bf16)
    context, log_total = attend_forward(queries, key_rows, values, segment, local_heads)
    attn_share = half_scatter(contract_cols(context, out_full))
    middle = residual + attn_share + norm_biases[2]
    second_out, normed_second, inv_second = normalize(middle, norm_gains[1], norm_biases[1])
    second_half = lax.all_gather(second_out.astype(bf16), "tensor", axis=0, tiled=True)
    hidden_pre = jnp.dot(second_half, in_full, preferred_element_type=jnp.float32) + in_bias
    gelu_value, gelu_slope = gelu_pair(hidden_pre)
    activation = gelu_value.astype(bf16)
    mlp_share = half_scatter(contract_cols(activation, back_full))
    block_out = (middle + mlp_share + norm_biases[3]).astype(bf16)
    cotangent = out_cotangent[0].astype(jnp.float32)
    grad_back_part = contract_rows(cotangent_full, activation)
    hidden_grad = jnp.dot(cotangent_full, back_full, preferred_element_type=jnp.float32) * gelu_slope
    hidden_half = hidden_grad.astype(bf16)
    grad_in_part = contract_rows(second_half, hidden_half)
    second_grad = half_scatter(contract_cols(hidden_half, in_full))
    middle_grad = cotangent + normalize_back(second_grad, normed_second, inv_second, norm_gains[1])
    middle_full = lax.all_gather(middle_grad.astype(bf16), "tensor", axis=0, tiled=True)
    grad_out_part = contract_rows(middle_full, context)
    context_grad = jnp.dot(middle_full, out_full, preferred_element_type=jnp.float32).astype(bf16)
    query_grad, key_grad, value_grad = attend_backward(
        queries, key_rows, values, segment, context, log_total, context_grad, local_heads
    )
    proj_half = jnp.concatenate([query_grad, key_grad, value_grad], axis=1).astype(bf16)
    grad_qkv_part = contract_rows(first_half, proj_half)
    first_grad = half_scatter(contract_cols(proj_half, qkv_full))
    input_grad = middle_grad + normalize_back(first_grad, normed_first, inv_first, norm_gains[0])
    parts = jnp.concatenate(
        [grad_qkv_part, grad_out_part, grad_in_part, grad_back_part], axis=1
    ).astype(bf16)
    grads = lax.psum_scatter(parts, "dp", scatter_dimension=0, tiled=True).astype(jnp.float32)
    grad_qkv = jnp.stack([grads[:, : cuts[0]], grads[:, cuts[0] : cuts[1]], grads[:, cuts[1] : cuts[2]]])
    grad_out = grads[:, cuts[2] : cuts[3]].T
    grad_in = grads[:, cuts[3] : cuts[4]]
    grad_back = grads[:, cuts[4] :].T
    own = jnp.concatenate(
        [jnp.sum(query_grad, axis=0), jnp.sum(value_grad, axis=0), jnp.sum(hidden_grad, axis=0)]
    )
    tensors = lax.axis_size("tensor")
    rank = lax.axis_index("tensor")
    spread = jnp.where(jnp.arange(tensors)[:, None] == rank, own[None], 0.0)
    norm_terms = jnp.stack(
        [
            jnp.sum(first_grad * normed_first, axis=0),
            jnp.sum(second_grad * normed_second, axis=0),
            jnp.sum(first_grad, axis=0),
            jnp.sum(second_grad, axis=0),
            jnp.sum(middle_grad, axis=0),
            jnp.sum(cotangent, axis=0),
        ]
    )
    total = lax.psum(
        jnp.concatenate([spread.reshape(-1), norm_terms.reshape(-1)]), ("dp", "tensor")
    )
    width = own.shape[0]
    own_total = lax.dynamic_slice(total, (rank * width,), (width,))
    norm_total = total[tensors * width :].reshape(norm_terms.shape)
    return (
        block_out[None],
        input_grad[None],
        grad_qkv,
        grad_out,
        grad_in,
        grad_back,
        own_total[: 2 * head_cols].reshape(2, head_cols),
        own_total[2 * head_cols :],
        norm_total[:2],
        norm_total[2:],
    )


def matmul(left, right):
    return jnp.dot(left, right, preferred_element_type=jnp.float32)


def layer_kernel(
    nt,
    nd,
    x_ref,
    seg_ref,
    wq_ref,
    wo_ref,
    wi_ref,
    wb_ref,
    cot_ref,
    qvb_ref,
    inb_ref,
    gains_ref,
    biases_ref,
    bo_ref,
    ig_ref,
    gq_ref,
    go_ref,
    gi_ref,
    gb_ref,
    sm_ref,
    fq,
    fo,
    fi,
    fb,
    first_ref,
    second_ref,
    cot_full,
    mid_full,
    segs,
    qs,
    ks,
    vs,
    ctx,
    probs,
    hb,
    act,
    hh,
    cg,
    ph,
    send,
    recv,
    own,
    mid,
    norm1,
    norm2,
    mgrad,
    pq,
    po,
    pi,
    pb,
    aq,
    ao,
    ai,
    ab,
    bq,
    bo,
    bi,
    bb,
    rq,
    ro,
    ri,
    rb,
    small,
    zsmall,
    psmall,
    csmall,
    csend,
    zs,
    zr,
    ds,
    dr,
):
    bf16 = jnp.bfloat16
    f32 = jnp.float32
    nc = nd // 2
    t = lax.axis_index("tensor")
    d = lax.axis_index("dp")
    core = lax.rem(d, 2)
    chip = d // 2
    partner = chip * 2 + 1 - core
    T, D = x_ref.shape
    rows = wq_ref.shape[0]
    E = ctx.shape[1]
    heads = E // HEAD
    seq = nt * T
    weights = ((wq_ref, fq), (wo_ref, fo), (wi_ref, fi), (wb_ref, fb))
    grads = (
        (pq, aq, bq, rq, gq_ref),
        (po, ao, bo, ro, go_ref),
        (pi, ai, bi, ri, gi_ref),
        (pb, ab, bb, rb, gb_ref),
    )

    def remote(src, dst, ssem, rsem, **where):
        return pltpu.make_async_remote_copy(
            src_ref=src,
            dst_ref=dst,
            send_sem=ssem,
            recv_sem=rsem,
            device_id=where,
            device_id_type=pl.DeviceIdType.MESH,
        )

    def blk(index, size=T):
        return pl.ds(pl.multiple_of(index * size, size), size)

    def other(k):
        return lax.rem(t + k, nt)

    def chip_at(k):
        return lax.rem(chip + k, nc)

    def zcopy(kind, k, src, dst):
        return remote(src, dst, zs.at[kind, k], zr.at[kind, t], tensor=other(k))

    def zwait(kind, k, dst):
        remote(dst, dst, zs.at[kind, 0], zr.at[kind, other(k)], tensor=other(k)).wait_recv()

    sent = []

    def go_send(copy):
        copy.start()
        sent.append(copy)

    def gather_send(kind, ref):
        for k in range(1, nt):
            go_send(zcopy(kind, k, ref.at[blk(t)], ref.at[blk(t)]))

    barrier = pltpu.get_barrier_semaphore()
    for k in range(1, nt):
        pl.semaphore_signal(
            barrier, inc=1, device_id={"tensor": other(k)}, device_id_type=pl.DeviceIdType.MESH
        )
    for k in range(1, nc):
        pl.semaphore_signal(
            barrier,
            inc=1,
            device_id={"dp": chip_at(k) * 2 + core},
            device_id_type=pl.DeviceIdType.MESH,
        )
    pl.semaphore_signal(
        barrier, inc=1, device_id={"dp": partner}, device_id_type=pl.DeviceIdType.MESH
    )
    pl.semaphore_wait(barrier, nt - 1 + nc - 1 + 1)

    def weight_send(w):
        src, full = weights[w]
        for k in range(1, nc):
            go_send(
                remote(
                    src,
                    full.at[blk(d, rows)],
                    ds.at[0, w, k],
                    dr.at[0, w, chip],
                    dp=chip_at(k) * 2 + core,
                )
            )
        go_send(
            remote(src, full.at[blk(d, rows)], ds.at[1, w, 0], dr.at[1, w, chip], dp=partner)
        )
        full[blk(d, rows), :] = src[...]

    def weight_pass(w):
        full = weights[w][1]
        for k in range(1, nc):
            c = chip_at(k)
            piece = full.at[blk(c * 2 + core, rows)]
            remote(piece, piece, ds.at[0, w, 0], dr.at[0, w, c], dp=c * 2 + core).wait_recv()
            go_send(remote(piece, piece, ds.at[1, w, k], dr.at[1, w, c], dp=partner))

    def weight_wait(w):
        full = weights[w][1]
        for k in range(nc):
            c = chip_at(k)
            piece = full.at[blk(c * 2 + 1 - core, rows)]
            remote(piece, piece, ds.at[1, w, 0], dr.at[1, w, c], dp=partner).wait_recv()

    weight_send(0)
    residual = x_ref[...].astype(f32)
    first_out, normed_first, inv_first = normalize(residual, gains_ref[0:1], biases_ref[0:1])
    norm1[...] = normed_first
    first_ref[blk(t), :] = first_out.astype(bf16)
    gather_send(0, first_ref)
    segs[t] = seg_ref[...]
    for k in range(1, nt):
        go_send(zcopy(1, k, seg_ref, segs.at[t]))
    for w in (1, 2, 3):
        weight_send(w)
    cot_full[blk(t), :] = cot_ref[...]
    for k in range(1, nt):
        go_send(zcopy(2, k, cot_ref, cot_full.at[blk(t)]))
    weight_pass(0)
    weight_wait(0)

    def project(s, carry):
        b = other(s)

        @pl.when(s > 0)
        def _():
            zwait(0, s, first_ref.at[blk(b)])

        out = matmul(first_ref[blk(b), :], fq[...])
        qs[blk(b), :] = (out[:, :E] + qvb_ref[0:1]).astype(bf16)
        ks[blk(b), :] = out[:, E : 2 * E].astype(bf16)
        vs[blk(b), :] = (out[:, 2 * E :] + qvb_ref[1:2]).astype(bf16)
        return carry

    lax.fori_loop(0, nt, project, 0)
    for k in range(1, nt):
        zwait(1, k, segs.at[other(k)])
    weight_pass(1)

    reach = (seq // 2 - 1 + T - 1) // T
    inv_root = 1.0 / math.sqrt(HEAD)
    for b in range(nt):
        low = max(0, b - reach)
        width = (b + 1 - low) * T
        key_seg = jnp.concatenate(
            [segs[j][0:1].astype(f32) for j in range(low, b + 1)], axis=1
        )
        query_seg = jnp.transpose(jnp.broadcast_to(segs[b][0:1].astype(f32), (T, T)))[:, 0:1]
        query_pos = lax.broadcasted_iota(jnp.int32, (T, width), 0) + b * T
        key_pos = lax.broadcasted_iota(jnp.int32, (T, width), 1) + low * T
        allowed = (key_pos <= query_pos) & (query_seg == key_seg)
        for h in range(heads):
            cols = slice(h * HEAD, (h + 1) * HEAD)
            scores = (
                contract_cols(qs[b * T : (b + 1) * T, cols], ks[low * T : (b + 1) * T, cols])
                * inv_root
            )
            scores = jnp.where(allowed, scores, -jnp.inf)
            row_max = jnp.max(scores, axis=-1, keepdims=True)
            log_total = row_max + jnp.log(
                jnp.sum(jnp.exp(scores - row_max), axis=-1, keepdims=True)
            )
            prob = jnp.exp(scores - log_total)
            probs[h, b, :, :width] = prob
            ctx[b * T : (b + 1) * T, cols] = matmul(
                prob.astype(bf16), vs[low * T : (b + 1) * T, cols]
            ).astype(bf16)
    weight_wait(1)

    def scatter(kind, slot, make):
        def step(s, carry):
            b = other(s + 1)
            share = make(b)

            @pl.when(s < nt - 1)
            def _():
                send[slot, b] = share.astype(bf16)
                zcopy(kind, s + 1, send.at[slot, b], recv.at[slot, t]).start()

            @pl.when(s == nt - 1)
            def _():
                own[slot] = share

            return carry

        lax.fori_loop(0, nt, step, 0)
        for k in range(1, nt):
            sent.append(zcopy(kind, k, send.at[slot, other(k)], recv.at[slot, t]))

    def scattered(kind, slot):
        total = own[slot]
        for k in range(1, nt):
            zwait(kind, k, recv.at[slot, other(k)])
            total = total + recv[slot, other(k)].astype(f32)
        return total

    scatter(5, 0, lambda b: contract_cols(ctx[blk(b), :], fo[...]))
    weight_pass(2)
    weight_pass(3)
    weight_wait(3)
    middle = residual + scattered(5, 0) + biases_ref[2:3]
    mid[...] = middle
    second_out, normed_second, inv_second = normalize(middle, gains_ref[1:2], biases_ref[1:2])
    norm2[...] = normed_second
    second_ref[blk(t), :] = second_out.astype(bf16)
    gather_send(3, second_ref)

    def back_step(s, carry):
        b = other(s)

        @pl.when(s > 0)
        def _():
            zwait(2, s, cot_full.at[blk(b)])

        hb[blk(b), :] = matmul(cot_full[blk(b), :], fb[...])
        return carry

    lax.fori_loop(0, nt, back_step, 0)
    weight_wait(2)
    small[...] = jnp.zeros_like(small)

    def hidden_step(s, carry):
        b = other(s)

        @pl.when(s > 0)
        def _():
            zwait(3, s, second_ref.at[blk(b)])

        pre = matmul(second_ref[blk(b), :], fi[...]) + inb_ref[...]
        value, slope = gelu_pair(pre)
        act[blk(b), :] = value.astype(bf16)
        grad = hb[blk(b), :] * slope
        small[8:9, : grad.shape[1]] += jnp.sum(grad, axis=0, keepdims=True)
        half = grad.astype(bf16)
        hh[blk(b), :] = half
        share = contract_cols(half, fi[...])

        @pl.when(s > 0)
        def _():
            send[1, b] = share.astype(bf16)
            zcopy(6, s, send.at[1, b], recv.at[1, t]).start()

        @pl.when(s == 0)
        def _():
            own[1] = share

        return carry

    lax.fori_loop(0, nt, hidden_step, 0)
    for k in range(1, nt):
        sent.append(zcopy(6, k, send.at[1, other(k)], recv.at[1, t]))
    scatter(7, 2, lambda b: contract_cols(act[blk(b), :], fb[...]))

    def weight_grad(w, left, right):
        part, first_recv = grads[w][0], grads[w][1]
        step = 128

        def chunk(c, carry):
            part[blk(c, step), :] = contract_rows(left[:, blk(c, step)], right[...]).astype(bf16)
            return carry

        lax.fori_loop(0, D // step, chunk, 0)
        for c in range(nc):
            go_send(
                remote(
                    part.at[blk(c * 2 + 1 - core, rows)],
                    first_recv.at[c],
                    ds.at[2, w, c],
                    dr.at[2, w, c],
                    dp=partner,
                )
            )

    def pair_sum(w, c):
        part, first_recv = grads[w][0], grads[w][1]
        piece = first_recv.at[c]
        remote(piece, piece, ds.at[2, w, 0], dr.at[2, w, c], dp=partner).wait_recv()
        return part[blk(c * 2 + core, rows), :].astype(f32) + first_recv[c].astype(f32)

    def grad_pass(w):
        pairs, second_recv, out = grads[w][2], grads[w][3], grads[w][4]
        for k in range(1, nc):
            c = chip_at(k)
            pairs[c] = pair_sum(w, c).astype(bf16)
            go_send(
                remote(
                    pairs.at[c],
                    second_recv.at[chip],
                    ds.at[3, w, k],
                    dr.at[3, w, chip],
                    dp=c * 2 + core,
                )
            )
        out[...] = pair_sum(w, chip)

    def grad_finish(w):
        second_recv, out = grads[w][3], grads[w][4]
        total = out[...]
        for k in range(1, nc):
            c = chip_at(k)
            piece = second_recv.at[c]
            remote(piece, piece, ds.at[3, w, 0], dr.at[3, w, c], dp=c * 2 + core).wait_recv()
            total = total + second_recv[c].astype(f32)
        out[...] = total

    weight_grad(2, second_ref, hh)
    second_grad = scattered(6, 1)
    cotangent = cot_ref[...].astype(f32)
    middle_grad = cotangent + normalize_back(second_grad, norm2[...], inv_second, gains_ref[1:2])
    mgrad[...] = middle_grad
    mid_full[blk(t), :] = middle_grad.astype(bf16)
    gather_send(4, mid_full)
    small[1:2, :] = jnp.sum(second_grad * norm2[...], axis=0, keepdims=True)
    small[3:4, :] = jnp.sum(second_grad, axis=0, keepdims=True)
    small[4:5, :] = jnp.sum(middle_grad, axis=0, keepdims=True)
    small[5:6, :] = jnp.sum(cotangent, axis=0, keepdims=True)
    weight_grad(3, cot_full, act)
    grad_pass(2)
    grad_pass(3)
    bo_ref[...] = (mid[...] + scattered(7, 2) + biases_ref[3:4]).astype(bf16)

    def context_step(s, carry):
        b = other(s)

        @pl.when(s > 0)
        def _():
            zwait(4, s, mid_full.at[blk(b)])

        cg[blk(b), :] = matmul(mid_full[blk(b), :], fo[...]).astype(bf16)
        return carry

    lax.fori_loop(0, nt, context_step, 0)

    for h in range(heads):
        cols = slice(h * HEAD, (h + 1) * HEAD)
        key_grads = [None] * nt
        value_grads = [None] * nt
        query_sum = 0.0
        for b in range(nt):
            low = max(0, b - reach)
            width = (b + 1 - low) * T
            here, window = slice(b * T, (b + 1) * T), slice(low * T, (b + 1) * T)
            prob = probs[h, b, :, :width]
            grad = cg[here, cols]
            prob_grad = contract_cols(grad, vs[window, cols])
            row_dot = jnp.sum(
                grad.astype(f32) * ctx[here, cols].astype(f32), axis=-1, keepdims=True
            )
            score_grad = (prob * (prob_grad - row_dot) * inv_root).astype(bf16)
            query_grad = matmul(score_grad, ks[window, cols])
            query_sum = query_sum + jnp.sum(query_grad, axis=0, keepdims=True)
            ph[here, h * HEAD : (h + 1) * HEAD] = query_grad.astype(bf16)
            key_part = contract_rows(score_grad, qs[here, cols])
            value_part = contract_rows(prob.astype(bf16), grad)
            for j in range(low, b + 1):
                at = slice((j - low) * T, (j - low + 1) * T)
                fresh = key_grads[j] is None
                key_grads[j] = key_part[at] if fresh else key_grads[j] + key_part[at]
                value_grads[j] = value_part[at] if fresh else value_grads[j] + value_part[at]
        value_sum = 0.0
        for j in range(nt):
            here = slice(j * T, (j + 1) * T)
            ph[here, E + h * HEAD : E + (h + 1) * HEAD] = key_grads[j].astype(bf16)
            ph[here, 2 * E + h * HEAD : 2 * E + (h + 1) * HEAD] = value_grads[j].astype(bf16)
            value_sum = value_sum + jnp.sum(value_grads[j], axis=0, keepdims=True)
        small[9:10, h * HEAD : (h + 1) * HEAD] = query_sum
        small[10:11, h * HEAD : (h + 1) * HEAD] = value_sum

    scatter(8, 3, lambda b: contract_cols(ph[blk(b), :], fq[...]))
    weight_grad(0, first_ref, ph)
    weight_grad(1, mid_full, ctx)
    grad_pass(0)
    grad_pass(1)
    first_grad = scattered(8, 3)
    ig_ref[...] = mgrad[...] + normalize_back(
        first_grad, norm1[...], inv_first, gains_ref[0:1]
    )
    small[0:1, :] = jnp.sum(first_grad * norm1[...], axis=0, keepdims=True)
    small[2:3, :] = jnp.sum(first_grad, axis=0, keepdims=True)
    zsmall[t] = small[0:8, :]
    for k in range(1, nt):
        go_send(zcopy(9, k, zsmall.at[t], zsmall.at[t]))
    for w in (2, 3):
        grad_finish(w)
    summed = small[0:8, :]
    for k in range(1, nt):
        zwait(9, k, zsmall.at[other(k)])
    summed = zsmall[0]
    for k in range(1, nt):
        summed = summed + zsmall[k]
    psmall[core] = jnp.concatenate([summed, small[8:16, :]], axis=0)
    go_send(
        remote(psmall.at[core], psmall.at[core], ds.at[2, 4, 0], dr.at[2, 4, 0], dp=partner)
    )
    piece = psmall.at[1 - core]
    remote(piece, piece, ds.at[2, 4, 1], dr.at[2, 4, 0], dp=partner).wait_recv()
    csmall[chip] = psmall[0] + psmall[1]
    for k in range(1, nc):
        go_send(
            remote(
                csmall.at[chip],
                csmall.at[chip],
                ds.at[3, 4, k],
                dr.at[3, 4, chip],
                dp=chip_at(k) * 2 + core,
            )
        )
    for w in (0, 1):
        grad_finish(w)
    for k in range(1, nc):
        c = chip_at(k)
        piece = csmall.at[c]
        remote(piece, piece, ds.at[3, 4, 0], dr.at[3, 4, c], dp=c * 2 + core).wait_recv()
    total = csmall[0]
    for c in range(1, nc):
        total = total + csmall[c]
    sm_ref[...] = total
    for copy in sent:
        copy.wait_send()


def kernel_shards(
    nt,
    nd,
    block_input,
    segment_ids,
    w_qkv,
    w_out,
    w_in,
    w_back,
    qv_bias,
    in_bias,
    norm_gains,
    norm_biases,
    out_cotangent,
):
    bf16, f32 = jnp.bfloat16, jnp.float32
    T, D = block_input.shape[1:]
    E, F = w_qkv.shape[2], w_in.shape[1]
    rows = D // nd
    seq = nt * T
    heads = E // HEAD
    nc = nd // 2
    reach = (seq // 2 - 1 + T - 1) // T
    window = min(nt, reach + 1) * T
    widths = (3 * E, E, F, F)
    wq = jnp.concatenate([w_qkv[0], w_qkv[1], w_qkv[2]], axis=1)
    seg = jnp.broadcast_to(segment_ids, (8, T))
    vm = pltpu.VMEM
    scratch = (
        [vm((D, n), bf16) for n in widths]
        + [vm((seq, D), bf16)] * 4
        + [vm((nt, 8, T), jnp.int32)]
        + [vm((seq, E), bf16)] * 4
        + [vm((heads, nt, T, window), f32)]
        + [vm((seq, F), f32), vm((seq, F), bf16), vm((seq, F), bf16)]
        + [vm((seq, E), bf16), vm((seq, 3 * E), bf16)]
        + [vm((4, nt, T, D), bf16)] * 2
        + [vm((4, T, D), f32)]
        + [vm((T, D), f32)] * 4
        + [vm((D, n), bf16) for n in widths]
        + [vm((nc, rows, n), bf16) for n in widths] * 3
        + [vm((16, D), f32), vm((nt, 8, D), f32), vm((2, 16, D), f32), vm((nc, 16, D), f32)]
        + [vm((8, 128), f32)]
        + [pltpu.SemaphoreType.DMA((10, nt))] * 2
        + [pltpu.SemaphoreType.DMA((4, 5, nc))] * 2
    )
    spec = pl.BlockSpec(memory_space=pltpu.VMEM)
    outs = pl.pallas_call(
        functools.partial(layer_kernel, nt, nd),
        out_shape=[
            jax.ShapeDtypeStruct((T, D), bf16),
            jax.ShapeDtypeStruct((T, D), f32),
            *[jax.ShapeDtypeStruct((rows, n), f32) for n in widths],
            jax.ShapeDtypeStruct((16, D), f32),
        ],
        in_specs=[spec] * 11,
        out_specs=[spec] * 7,
        scratch_shapes=scratch,
        compiler_params=pltpu.CompilerParams(
            collective_id=0, has_side_effects=True, vmem_limit_bytes=60 * 1024 * 1024
        ),
        name="layer",
    )(
        block_input[0],
        seg,
        wq,
        w_out.T,
        w_in,
        w_back.T,
        out_cotangent[0],
        qv_bias,
        in_bias[None],
        norm_gains,
        norm_biases,
    )
    block_out, input_grad, gq, go, gi, gb, total = outs
    return (
        block_out[None],
        input_grad[None],
        jnp.stack([gq[:, :E], gq[:, E : 2 * E], gq[:, 2 * E :]]),
        go.T,
        gi,
        gb.T,
        total[9:11, :E],
        total[8, :F],
        total[:2],
        total[2:6],
    )


def solution(mesh):
    in_specs = (
        P("dp", "tensor", None),
        P("dp", "tensor"),
        P(None, "dp", "tensor"),
        P("tensor", "dp"),
        P("dp", "tensor"),
        P("tensor", "dp"),
        P(None, "tensor"),
        P("tensor"),
        P(),
        P(),
        P("dp", "tensor", None),
    )
    out_specs = (
        P("dp", "tensor", None),
        P("dp", "tensor", None),
        P(None, "dp", "tensor"),
        P("tensor", "dp"),
        P("dp", "tensor"),
        P("tensor", "dp"),
        P(None, "tensor"),
        P("tensor"),
        P(),
        P(),
    )
    nt, nd = mesh.shape["tensor"], mesh.shape["dp"]

    def body(*args):
        block_input, w_qkv, w_in = args[0], args[2], args[4]
        tokens, features = block_input.shape[1:]
        fits = (
            nd % 2 == 0
            and w_in.shape[0] % 16 == 0
            and tokens % 128 == 0
            and features % 128 == 0
            and w_in.shape[1] <= features
            and w_qkv.shape[2] % HEAD == 0
        )
        if fits:
            return kernel_shards(nt, nd, *args)
        return shards(*args)

    return jax.shard_map(body, mesh=mesh, in_specs=in_specs, out_specs=out_specs, check_vma=False)
```

```python
import functools
import math

import jax
import jax.numpy as jnp
from jax import lax
from jax.experimental import pallas as pl
from jax.experimental.pallas import tpu as pltpu
from jax.sharding import PartitionSpec as P

HEAD = 64


EPS = 1e-05
GELU_C = math.sqrt(2.0 / math.pi)
GELU_A = 0.044715


def normalize(residual, gain_row, offset_row):
    centered = residual - jnp.mean(residual, axis=-1, keepdims=True)
    inv_std = lax.rsqrt(jnp.mean(centered * centered, axis=-1, keepdims=True) + EPS)
    normed = centered * inv_std
    return (normed * gain_row + offset_row, normed, inv_std)


def normalize_back(upstream, normed, inv_std, gain_row):
    scaled = upstream * gain_row
    return inv_std * (
        scaled
        - jnp.mean(scaled, axis=-1, keepdims=True)
        - normed * jnp.mean(scaled * normed, axis=-1, keepdims=True)
    )


def gelu_pair(inputs):
    inner_arg = GELU_C * (inputs + GELU_A * inputs * inputs * inputs)
    tangent_h = jnp.tanh(inner_arg)
    value_out = 0.5 * inputs * (1.0 + tangent_h)
    slope_out = 0.5 * (1.0 + tangent_h) + 0.5 * inputs * (1.0 - tangent_h * tangent_h) * GELU_C * (
        1.0 + 3.0 * GELU_A * inputs * inputs
    )
    return (value_out, slope_out)


def contract_rows(left, right):
    return lax.dot_general(
        left, right, (((0,), (0,)), ((), ())), preferred_element_type=jnp.float32
    )


def contract_cols(left, right):
    return lax.dot_general(
        left, right, (((1,), (1,)), ((), ())), preferred_element_type=jnp.float32
    )


def masked_scores(query_block, key_rows, segment, key_end, num_heads):
    block_rows = query_block.shape[0]
    width = query_block.shape[1] // num_heads
    query_heads = query_block.reshape(block_rows, num_heads, width)
    key_heads = key_rows.reshape(key_end, num_heads, width)
    raw_scores = jnp.einsum(
        "qhd,khd->hqk", query_heads, key_heads, preferred_element_type=jnp.float32
    ) * (1.0 / math.sqrt(width))
    query_pos = jnp.arange(block_rows, dtype=jnp.int32)
    key_pos = jnp.arange(key_end, dtype=jnp.int32)
    allowed = (key_pos[None, :] <= query_pos[:, None]) & (segment[None, :] == segment[:, None])
    return jnp.where(allowed[None], raw_scores, -jnp.inf)


def attend_forward(queries, key_rows, values, segment, num_heads):
    total_rows = queries.shape[0]
    block_rows = min(512, total_rows)
    width = queries.shape[1] // num_heads
    scores = masked_scores(queries, key_rows, segment, block_rows, num_heads)
    row_max = jnp.max(scores, axis=-1, keepdims=True)
    log_total = row_max + jnp.log(jnp.sum(jnp.exp(scores - row_max), axis=-1, keepdims=True))
    weights = jnp.exp(scores - log_total).astype(jnp.bfloat16)
    value_heads = values.reshape(block_rows, num_heads, width)
    context = jnp.einsum("hqk,khd->qhd", weights, value_heads, preferred_element_type=jnp.float32)
    contexts = context.reshape(block_rows, num_heads * width).astype(jnp.bfloat16)
    return (contexts, log_total)


def attend_backward(
    queries, key_rows, values, segment, context, log_total, context_grad, num_heads
):
    total_rows = queries.shape[0]
    block_rows = min(512, total_rows)
    width = queries.shape[1] // num_heads
    inv_root = 1.0 / math.sqrt(width)
    key_grad = jnp.zeros((total_rows, num_heads, width), jnp.float32)
    value_grad = jnp.zeros((total_rows, num_heads, width), jnp.float32)
    scores = masked_scores(queries, key_rows, segment, block_rows, num_heads)
    probs = jnp.exp(scores - log_total)
    probs_half = probs.astype(jnp.bfloat16)
    grad_heads = context_grad.reshape(block_rows, num_heads, width)
    context_heads = context.reshape(block_rows, num_heads, width)
    value_heads = values.reshape(block_rows, num_heads, width)
    key_heads = key_rows.reshape(block_rows, num_heads, width)
    query_heads = queries.reshape(block_rows, num_heads, width)
    prob_grad = jnp.einsum(
        "qhd,khd->hqk", grad_heads, value_heads, preferred_element_type=jnp.float32
    )
    row_dot = jnp.transpose(
        jnp.sum(grad_heads.astype(jnp.float32) * context_heads.astype(jnp.float32), axis=-1)
    )[:, :, None]
    score_grad = (probs * (prob_grad - row_dot) * inv_root).astype(jnp.bfloat16)
    query_grads = jnp.einsum(
        "hqk,khd->qhd", score_grad, key_heads, preferred_element_type=jnp.float32
    ).reshape(block_rows, num_heads * width)
    key_grad = key_grad.at[:block_rows].add(
        jnp.einsum("hqk,qhd->khd", score_grad, query_heads, preferred_element_type=jnp.float32)
    )
    value_grad = value_grad.at[:block_rows].add(
        jnp.einsum("hqk,qhd->khd", probs_half, grad_heads, preferred_element_type=jnp.float32)
    )
    return (
        query_grads,
        key_grad.reshape(total_rows, num_heads * width),
        value_grad.reshape(total_rows, num_heads * width),
    )


def half_scatter(share):
    return lax.psum_scatter(
        share.astype(jnp.bfloat16), "tensor", scatter_dimension=0, tiled=True
    ).astype(jnp.float32)


def shards(
    block_input,
    segment_ids,
    w_qkv,
    w_out,
    w_in,
    w_back,
    qv_bias,
    in_bias,
    norm_gains,
    norm_biases,
    out_cotangent,
):
    bf16 = jnp.bfloat16
    residual = block_input[0].astype(jnp.float32)
    head_cols = w_qkv.shape[2]
    hidden_cols = w_in.shape[1]
    local_heads = head_cols // HEAD
    cuts = [head_cols, 2 * head_cols, 3 * head_cols, 4 * head_cols, 4 * head_cols + hidden_cols]
    packed = jnp.concatenate([w_qkv[0], w_qkv[1], w_qkv[2], w_out.T, w_in, w_back.T], axis=1)
    full = lax.all_gather(packed, "dp", axis=0, tiled=True)
    qkv_full = full[:, : cuts[2]]
    out_full = full[:, cuts[2] : cuts[3]]
    in_full = full[:, cuts[3] : cuts[4]]
    back_full = full[:, cuts[4] :]
    first_out, normed_first, inv_first = normalize(residual, norm_gains[0], norm_biases[0])
    first_half, segment, cotangent_full = (
        lax.all_gather(first_out.astype(bf16), "tensor", axis=0, tiled=True),
        lax.all_gather(segment_ids[0], "tensor", axis=0, tiled=True),
        lax.all_gather(out_cotangent[0], "tensor", axis=0, tiled=True),
    )
    projected = jnp.dot(first_half, qkv_full, preferred_element_type=jnp.float32)
    queries = (projected[:, : cuts[0]] + qv_bias[0]).astype(bf16)
    key_rows = projected[:, cuts[0] : cuts[1]].astype(bf16)
    values = (projected[:, cuts[1] :] + qv_bias[1]).astype(bf16)
    context, log_total = attend_forward(queries, key_rows, values, segment, local_heads)
    attn_share = half_scatter(contract_cols(context, out_full))
    middle = residual + attn_share + norm_biases[2]
    second_out, normed_second, inv_second = normalize(middle, norm_gains[1], norm_biases[1])
    second_half = lax.all_gather(second_out.astype(bf16), "tensor", axis=0, tiled=True)
    hidden_pre = jnp.dot(second_half, in_full, preferred_element_type=jnp.float32) + in_bias
    gelu_value, gelu_slope = gelu_pair(hidden_pre)
    activation = gelu_value.astype(bf16)
    mlp_share = half_scatter(contract_cols(activation, back_full))
    block_out = (middle + mlp_share + norm_biases[3]).astype(bf16)
    cotangent = out_cotangent[0].astype(jnp.float32)
    grad_back_part = contract_rows(cotangent_full, activation)
    hidden_grad = jnp.dot(cotangent_full, back_full, preferred_element_type=jnp.float32) * gelu_slope
    hidden_half = hidden_grad.astype(bf16)
    grad_in_part = contract_rows(second_half, hidden_half)
    second_grad = half_scatter(contract_cols(hidden_half, in_full))
    middle_grad = cotangent + normalize_back(second_grad, normed_second, inv_second, norm_gains[1])
    middle_full = lax.all_gather(middle_grad.astype(bf16), "tensor", axis=0, tiled=True)
    grad_out_part = contract_rows(middle_full, context)
    context_grad = jnp.dot(middle_full, out_full, preferred_element_type=jnp.float32).astype(bf16)
    query_grad, key_grad, value_grad = attend_backward(
        queries, key_rows, values, segment, context, log_total, context_grad, local_heads
    )
    proj_half = jnp.concatenate([query_grad, key_grad, value_grad], axis=1).astype(bf16)
    grad_qkv_part = contract_rows(first_half, proj_half)
    first_grad = half_scatter(contract_cols(proj_half, qkv_full))
    input_grad = middle_grad + normalize_back(first_grad, normed_first, inv_first, norm_gains[0])
    parts = jnp.concatenate(
        [grad_qkv_part, grad_out_part, grad_in_part, grad_back_part], axis=1
    ).astype(bf16)
    grads = lax.psum_scatter(parts, "dp", scatter_dimension=0, tiled=True).astype(jnp.float32)
    grad_qkv = jnp.stack([grads[:, : cuts[0]], grads[:, cuts[0] : cuts[1]], grads[:, cuts[1] : cuts[2]]])
    grad_out = grads[:, cuts[2] : cuts[3]].T
    grad_in = grads[:, cuts[3] : cuts[4]]
    grad_back = grads[:, cuts[4] :].T
    own = jnp.concatenate(
        [jnp.sum(query_grad, axis=0), jnp.sum(value_grad, axis=0), jnp.sum(hidden_grad, axis=0)]
    )
    tensors = lax.axis_size("tensor")
    rank = lax.axis_index("tensor")
    spread = jnp.where(jnp.arange(tensors)[:, None] == rank, own[None], 0.0)
    norm_terms = jnp.stack(
        [
            jnp.sum(first_grad * normed_first, axis=0),
            jnp.sum(second_grad * normed_second, axis=0),
            jnp.sum(first_grad, axis=0),
            jnp.sum(second_grad, axis=0),
            jnp.sum(middle_grad, axis=0),
            jnp.sum(cotangent, axis=0),
        ]
    )
    total = lax.psum(
        jnp.concatenate([spread.reshape(-1), norm_terms.reshape(-1)]), ("dp", "tensor")
    )
    width = own.shape[0]
    own_total = lax.dynamic_slice(total, (rank * width,), (width,))
    norm_total = total[tensors * width :].reshape(norm_terms.shape)
    return (
        block_out[None],
        input_grad[None],
        grad_qkv,
        grad_out,
        grad_in,
        grad_back,
        own_total[: 2 * head_cols].reshape(2, head_cols),
        own_total[2 * head_cols :],
        norm_total[:2],
        norm_total[2:],
    )


def matmul(left, right):
    return jnp.dot(left, right, preferred_element_type=jnp.float32)


def layer_kernel(
    nt,
    nd,
    x_ref,
    seg_ref,
    wq_ref,
    wo_ref,
    wi_ref,
    wb_ref,
    cot_ref,
    qvb_ref,
    inb_ref,
    gains_ref,
    biases_ref,
    bo_ref,
    ig_ref,
    gq_ref,
    go_ref,
    gi_ref,
    gb_ref,
    gqv_ref,
    ginb_ref,
    ggain_ref,
    gbias_ref,
    fq,
    fo,
    fi,
    fb,
    first_ref,
    second_ref,
    cot_full,
    mid_full,
    segs,
    qs,
    ks,
    vs,
    ctx,
    probs,
    hb,
    act,
    hh,
    cg,
    ph,
    send,
    recv,
    own,
    mid,
    norm1,
    norm2,
    mgrad,
    pq,
    po,
    pi,
    pb,
    aq,
    ao,
    ai,
    ab,
    bq,
    bo,
    bi,
    bb,
    rq,
    ro,
    ri,
    rb,
    small,
    zsmall,
    psmall,
    csmall,
    oq,
    oo,
    ob,
    zs,
    zr,
    ds,
    dr,
):
    bf16 = jnp.bfloat16
    f32 = jnp.float32
    nc = nd // 2
    t = lax.axis_index("tensor")
    d = lax.axis_index("dp")
    core = lax.rem(d, 2)
    chip = d // 2
    partner = chip * 2 + 1 - core
    T, D = x_ref.shape
    rows = wq_ref.shape[0]
    E = ctx.shape[1]
    heads = E // HEAD
    seq = nt * T
    weights = ((wq_ref, fq), (wo_ref, fo), (wi_ref, fi), (wb_ref, fb))
    grads = (
        (pq, aq, bq, rq, oq),
        (po, ao, bo, ro, oo),
        (pi, ai, bi, ri, gi_ref),
        (pb, ab, bb, rb, ob),
    )

    def remote(src, dst, ssem, rsem, **where):
        return pltpu.make_async_remote_copy(
            src_ref=src,
            dst_ref=dst,
            send_sem=ssem,
            recv_sem=rsem,
            device_id=where,
            device_id_type=pl.DeviceIdType.MESH,
        )

    def blk(index, size=T):
        return pl.ds(pl.multiple_of(index * size, size), size)

    def other(k):
        return lax.rem(t + k, nt)

    def chip_at(k):
        return lax.rem(chip + k, nc)

    def zcopy(kind, k, src, dst):
        return remote(src, dst, zs.at[kind, k], zr.at[kind, t], tensor=other(k))

    def zwait(kind, k, dst):
        remote(dst, dst, zs.at[kind, 0], zr.at[kind, other(k)], tensor=other(k)).wait_recv()

    sent = []

    def go_send(copy):
        copy.start()
        sent.append(copy)

    def gather_send(kind, ref):
        for k in range(1, nt):
            go_send(zcopy(kind, k, ref.at[blk(t)], ref.at[blk(t)]))

    barrier = pltpu.get_barrier_semaphore()
    for k in range(1, nt):
        pl.semaphore_signal(
            barrier, inc=1, device_id={"tensor": other(k)}, device_id_type=pl.DeviceIdType.MESH
        )
    for k in range(1, nc):
        pl.semaphore_signal(
            barrier,
            inc=1,
            device_id={"dp": chip_at(k) * 2 + core},
            device_id_type=pl.DeviceIdType.MESH,
        )
    pl.semaphore_signal(
        barrier, inc=1, device_id={"dp": partner}, device_id_type=pl.DeviceIdType.MESH
    )
    pl.semaphore_wait(barrier, nt - 1 + nc - 1 + 1)

    def weight_send(w):
        src, full = weights[w]
        for k in range(1, nc):
            go_send(
                remote(
                    src,
                    full.at[blk(d, rows)],
                    ds.at[0, w, k],
                    dr.at[0, w, chip],
                    dp=chip_at(k) * 2 + core,
                )
            )
        go_send(
            remote(src, full.at[blk(d, rows)], ds.at[1, w, 0], dr.at[1, w, chip], dp=partner)
        )
        full[blk(d, rows), :] = src[...]

    def weight_pass(w):
        full = weights[w][1]
        for k in range(1, nc):
            c = chip_at(k)
            piece = full.at[blk(c * 2 + core, rows)]
            remote(piece, piece, ds.at[0, w, 0], dr.at[0, w, c], dp=c * 2 + core).wait_recv()
            go_send(remote(piece, piece, ds.at[1, w, k], dr.at[1, w, c], dp=partner))

    def weight_wait(w):
        full = weights[w][1]
        for k in range(nc):
            c = chip_at(k)
            piece = full.at[blk(c * 2 + 1 - core, rows)]
            remote(piece, piece, ds.at[1, w, 0], dr.at[1, w, c], dp=partner).wait_recv()

    weight_send(0)
    residual = x_ref[...].astype(f32)
    first_out, normed_first, inv_first = normalize(residual, gains_ref[0:1], biases_ref[0:1])
    norm1[...] = normed_first
    first_ref[blk(t), :] = first_out.astype(bf16)
    gather_send(0, first_ref)
    segs[t] = seg_ref[...]
    for k in range(1, nt):
        go_send(zcopy(1, k, seg_ref, segs.at[t]))
    for w in (1, 2, 3):
        weight_send(w)
    cot_full[blk(t), :] = cot_ref[...]
    for k in range(1, nt):
        go_send(zcopy(2, k, cot_ref, cot_full.at[blk(t)]))
    weight_pass(0)
    weight_wait(0)

    def project(s, carry):
        b = other(s)

        @pl.when(s > 0)
        def _():
            zwait(0, s, first_ref.at[blk(b)])

        out = matmul(first_ref[blk(b), :], fq[...])
        qs[blk(b), :] = (out[:, :E] + qvb_ref[0:1]).astype(bf16)
        ks[blk(b), :] = out[:, E : 2 * E].astype(bf16)
        vs[blk(b), :] = (out[:, 2 * E :] + qvb_ref[1:2]).astype(bf16)
        return carry

    lax.fori_loop(0, nt, project, 0)
    for k in range(1, nt):
        zwait(1, k, segs.at[other(k)])
    weight_pass(1)

    reach = (seq // 2 - 1 + T - 1) // T
    inv_root = 1.0 / math.sqrt(HEAD)
    for b in range(nt):
        low = max(0, b - reach)
        width = (b + 1 - low) * T
        key_seg = jnp.concatenate(
            [segs[j][0:1].astype(f32) for j in range(low, b + 1)], axis=1
        )
        query_seg = jnp.transpose(jnp.broadcast_to(segs[b][0:1].astype(f32), (T, T)))[:, 0:1]
        query_pos = lax.broadcasted_iota(jnp.int32, (T, width), 0) + b * T
        key_pos = lax.broadcasted_iota(jnp.int32, (T, width), 1) + low * T
        allowed = (key_pos <= query_pos) & (query_seg == key_seg)
        for h in range(heads):
            cols = slice(h * HEAD, (h + 1) * HEAD)
            scores = (
                contract_cols(qs[b * T : (b + 1) * T, cols], ks[low * T : (b + 1) * T, cols])
                * inv_root
            )
            scores = jnp.where(allowed, scores, -jnp.inf)
            row_max = jnp.max(scores, axis=-1, keepdims=True)
            log_total = row_max + jnp.log(
                jnp.sum(jnp.exp(scores - row_max), axis=-1, keepdims=True)
            )
            prob = jnp.exp(scores - log_total)
            probs[h, b, :, :width] = prob
            ctx[b * T : (b + 1) * T, cols] = matmul(
                prob.astype(bf16), vs[low * T : (b + 1) * T, cols]
            ).astype(bf16)
    weight_wait(1)

    def scatter(kind, slot, make):
        def step(s, carry):
            b = other(s + 1)
            share = make(b)

            @pl.when(s < nt - 1)
            def _():
                send[slot, b] = share.astype(bf16)
                zcopy(kind, s + 1, send.at[slot, b], recv.at[slot, t]).start()

            @pl.when(s == nt - 1)
            def _():
                own[slot] = share

            return carry

        lax.fori_loop(0, nt, step, 0)
        for k in range(1, nt):
            sent.append(zcopy(kind, k, send.at[slot, other(k)], recv.at[slot, t]))

    def scattered(kind, slot):
        total = own[slot]
        for k in range(1, nt):
            zwait(kind, k, recv.at[slot, other(k)])
            total = total + recv[slot, other(k)].astype(f32)
        return total

    scatter(5, 0, lambda b: contract_cols(ctx[blk(b), :], fo[...]))
    weight_pass(2)
    weight_pass(3)
    weight_wait(3)
    middle = residual + scattered(5, 0) + biases_ref[2:3]
    mid[...] = middle
    second_out, normed_second, inv_second = normalize(middle, gains_ref[1:2], biases_ref[1:2])
    norm2[...] = normed_second
    second_ref[blk(t), :] = second_out.astype(bf16)
    gather_send(3, second_ref)

    def back_step(s, carry):
        b = other(s)

        @pl.when(s > 0)
        def _():
            zwait(2, s, cot_full.at[blk(b)])

        hb[blk(b), :] = matmul(cot_full[blk(b), :], fb[...])
        return carry

    lax.fori_loop(0, nt, back_step, 0)
    weight_wait(2)
    small[...] = jnp.zeros_like(small)

    def hidden_step(s, carry):
        b = other(s)

        @pl.when(s > 0)
        def _():
            zwait(3, s, second_ref.at[blk(b)])

        pre = matmul(second_ref[blk(b), :], fi[...]) + inb_ref[...]
        value, slope = gelu_pair(pre)
        act[blk(b), :] = value.astype(bf16)
        grad = hb[blk(b), :] * slope
        small[8:9, : grad.shape[1]] += jnp.sum(grad, axis=0, keepdims=True)
        half = grad.astype(bf16)
        hh[blk(b), :] = half
        share = contract_cols(half, fi[...])

        @pl.when(s > 0)
        def _():
            send[1, b] = share.astype(bf16)
            zcopy(6, s, send.at[1, b], recv.at[1, t]).start()

        @pl.when(s == 0)
        def _():
            own[1] = share

        return carry

    lax.fori_loop(0, nt, hidden_step, 0)
    for k in range(1, nt):
        sent.append(zcopy(6, k, send.at[1, other(k)], recv.at[1, t]))

    def weight_grad(w, left, right):
        part, first_recv = grads[w][0], grads[w][1]
        step = 128

        def chunk(c, carry):
            part[blk(c, step), :] = contract_rows(left[:, blk(c, step)], right[...]).astype(bf16)
            return carry

        lax.fori_loop(0, D // step, chunk, 0)
        for c in range(nc):
            go_send(
                remote(
                    part.at[blk(c * 2 + 1 - core, rows)],
                    first_recv.at[c],
                    ds.at[2, w, c],
                    dr.at[2, w, c],
                    dp=partner,
                )
            )

    def pair_sum(w, c):
        part, first_recv = grads[w][0], grads[w][1]
        piece = first_recv.at[c]
        remote(piece, piece, ds.at[2, w, 0], dr.at[2, w, c], dp=partner).wait_recv()
        return part[blk(c * 2 + core, rows), :].astype(f32) + first_recv[c].astype(f32)

    def grad_pass(w):
        pairs, second_recv, out = grads[w][2], grads[w][3], grads[w][4]
        for k in range(1, nc):
            c = chip_at(k)
            pairs[c] = pair_sum(w, c).astype(bf16)
            go_send(
                remote(
                    pairs.at[c],
                    second_recv.at[chip],
                    ds.at[3, w, k],
                    dr.at[3, w, chip],
                    dp=c * 2 + core,
                )
            )
        out[...] = pair_sum(w, chip)

    def grad_finish(w):
        second_recv, out = grads[w][3], grads[w][4]
        total = out[...]
        for k in range(1, nc):
            c = chip_at(k)
            piece = second_recv.at[c]
            remote(piece, piece, ds.at[3, w, 0], dr.at[3, w, c], dp=c * 2 + core).wait_recv()
            total = total + second_recv[c].astype(f32)
        if w == 0:
            for c in range(3):
                gq_ref[c] = total[:, c * E : (c + 1) * E]
        elif w == 1:
            go_ref[...] = jnp.transpose(total)
        elif w == 2:
            gi_ref[...] = total
        else:
            gb_ref[...] = total

    weight_grad(2, second_ref, hh)
    second_grad = scattered(6, 1)
    cotangent = cot_ref[...].astype(f32)
    middle_grad = cotangent + normalize_back(second_grad, norm2[...], inv_second, gains_ref[1:2])
    mgrad[...] = middle_grad
    mid_full[blk(t), :] = middle_grad.astype(bf16)
    gather_send(4, mid_full)
    small[1:2, :] = jnp.sum(second_grad * norm2[...], axis=0, keepdims=True)
    small[3:4, :] = jnp.sum(second_grad, axis=0, keepdims=True)
    small[4:5, :] = jnp.sum(middle_grad, axis=0, keepdims=True)
    small[5:6, :] = jnp.sum(cotangent, axis=0, keepdims=True)
    weight_grad(3, cot_full, act)
    scatter(7, 2, lambda b: contract_cols(act[blk(b), :], fb[...]))
    grad_pass(2)
    grad_pass(3)

    def context_step(s, carry):
        b = other(s)

        @pl.when(s > 0)
        def _():
            zwait(4, s, mid_full.at[blk(b)])

        cg[blk(b), :] = matmul(mid_full[blk(b), :], fo[...]).astype(bf16)
        return carry

    lax.fori_loop(0, nt, context_step, 0)

    for h in range(heads):
        cols = slice(h * HEAD, (h + 1) * HEAD)
        key_grads = [None] * nt
        value_grads = [None] * nt
        query_sum = 0.0
        for b in range(nt):
            low = max(0, b - reach)
            width = (b + 1 - low) * T
            here, window = slice(b * T, (b + 1) * T), slice(low * T, (b + 1) * T)
            prob = probs[h, b, :, :width]
            grad = cg[here, cols]
            prob_grad = contract_cols(grad, vs[window, cols])
            row_dot = jnp.sum(
                grad.astype(f32) * ctx[here, cols].astype(f32), axis=-1, keepdims=True
            )
            score_grad = (prob * (prob_grad - row_dot) * inv_root).astype(bf16)
            query_grad = matmul(score_grad, ks[window, cols])
            query_sum = query_sum + jnp.sum(query_grad, axis=0, keepdims=True)
            ph[here, h * HEAD : (h + 1) * HEAD] = query_grad.astype(bf16)
            key_part = contract_rows(score_grad, qs[here, cols])
            value_part = contract_rows(prob.astype(bf16), grad)
            for j in range(low, b + 1):
                at = slice((j - low) * T, (j - low + 1) * T)
                fresh = key_grads[j] is None
                key_grads[j] = key_part[at] if fresh else key_grads[j] + key_part[at]
                value_grads[j] = value_part[at] if fresh else value_grads[j] + value_part[at]
        value_sum = 0.0
        for j in range(nt):
            here = slice(j * T, (j + 1) * T)
            ph[here, E + h * HEAD : E + (h + 1) * HEAD] = key_grads[j].astype(bf16)
            ph[here, 2 * E + h * HEAD : 2 * E + (h + 1) * HEAD] = value_grads[j].astype(bf16)
            value_sum = value_sum + jnp.sum(value_grads[j], axis=0, keepdims=True)
        small[9:10, h * HEAD : (h + 1) * HEAD] = query_sum
        small[10:11, h * HEAD : (h + 1) * HEAD] = value_sum

    scatter(8, 3, lambda b: contract_cols(ph[blk(b), :], fq[...]))
    weight_grad(0, first_ref, ph)
    weight_grad(1, mid_full, ctx)
    grad_pass(0)
    grad_pass(1)
    bo_ref[...] = (mid[...] + scattered(7, 2) + biases_ref[3:4]).astype(bf16)
    for w in (2, 3):
        grad_finish(w)
    first_grad = scattered(8, 3)
    ig_ref[...] = mgrad[...] + normalize_back(
        first_grad, norm1[...], inv_first, gains_ref[0:1]
    )
    small[0:1, :] = jnp.sum(first_grad * norm1[...], axis=0, keepdims=True)
    small[2:3, :] = jnp.sum(first_grad, axis=0, keepdims=True)
    zsmall[t] = small[0:8, :]
    for k in range(1, nt):
        go_send(zcopy(9, k, zsmall.at[t], zsmall.at[t]))
    for k in range(1, nt):
        zwait(9, k, zsmall.at[other(k)])
    summed = zsmall[0]
    for k in range(1, nt):
        summed = summed + zsmall[k]
    psmall[core] = jnp.concatenate([summed, small[8:16, :]], axis=0)
    go_send(
        remote(psmall.at[core], psmall.at[core], ds.at[2, 4, 0], dr.at[2, 4, 0], dp=partner)
    )
    piece = psmall.at[1 - core]
    remote(piece, piece, ds.at[2, 4, 1], dr.at[2, 4, 0], dp=partner).wait_recv()
    csmall[chip] = psmall[0] + psmall[1]
    for k in range(1, nc):
        go_send(
            remote(
                csmall.at[chip],
                csmall.at[chip],
                ds.at[3, 4, k],
                dr.at[3, 4, chip],
                dp=chip_at(k) * 2 + core,
            )
        )
    for w in (0, 1):
        grad_finish(w)
    for k in range(1, nc):
        c = chip_at(k)
        piece = csmall.at[c]
        remote(piece, piece, ds.at[3, 4, 0], dr.at[3, 4, c], dp=c * 2 + core).wait_recv()
    total = csmall[0]
    for c in range(1, nc):
        total = total + csmall[c]
    gqv_ref[...] = total[9:11, :E]
    ginb_ref[...] = total[8:9, : inb_ref.shape[1]]
    ggain_ref[...] = total[0:2]
    gbias_ref[...] = total[2:6]
    for copy in sent:
        copy.wait_send()


def kernel_shards(
    nt,
    nd,
    block_input,
    segment_ids,
    w_qkv,
    w_out,
    w_in,
    w_back,
    qv_bias,
    in_bias,
    norm_gains,
    norm_biases,
    out_cotangent,
):
    bf16, f32 = jnp.bfloat16, jnp.float32
    T, D = block_input.shape[1:]
    E, F = w_qkv.shape[2], w_in.shape[1]
    rows = D // nd
    seq = nt * T
    heads = E // HEAD
    nc = nd // 2
    reach = (seq // 2 - 1 + T - 1) // T
    window = min(nt, reach + 1) * T
    widths = (3 * E, E, F, F)
    wq = jnp.concatenate([w_qkv[0], w_qkv[1], w_qkv[2]], axis=1)
    seg = jnp.broadcast_to(segment_ids, (8, T))
    vm = pltpu.VMEM
    scratch = (
        [vm((D, n), bf16) for n in widths]
        + [vm((seq, D), bf16)] * 4
        + [vm((nt, 8, T), jnp.int32)]
        + [vm((seq, E), bf16)] * 4
        + [vm((heads, nt, T, window), f32)]
        + [vm((seq, F), f32), vm((seq, F), bf16), vm((seq, F), bf16)]
        + [vm((seq, E), bf16), vm((seq, 3 * E), bf16)]
        + [vm((4, nt, T, D), bf16)] * 2
        + [vm((4, T, D), f32)]
        + [vm((T, D), f32)] * 4
        + [vm((D, n), bf16) for n in widths]
        + [vm((nc, rows, n), bf16) for n in widths] * 3
        + [vm((16, D), f32), vm((nt, 8, D), f32), vm((2, 16, D), f32), vm((nc, 16, D), f32)]
        + [vm((rows, n), f32) for n in (3 * E, E, F)]
        + [pltpu.SemaphoreType.DMA((10, nt))] * 2
        + [pltpu.SemaphoreType.DMA((4, 5, nc))] * 2
    )
    spec = pl.BlockSpec(memory_space=pltpu.VMEM)
    outs = pl.pallas_call(
        functools.partial(layer_kernel, nt, nd),
        out_shape=[
            jax.ShapeDtypeStruct((T, D), bf16),
            jax.ShapeDtypeStruct((T, D), f32),
            jax.ShapeDtypeStruct((3, rows, E), f32),
            jax.ShapeDtypeStruct((E, rows), f32),
            jax.ShapeDtypeStruct((rows, F), f32),
            jax.ShapeDtypeStruct((rows, F), f32),
            jax.ShapeDtypeStruct((2, E), f32),
            jax.ShapeDtypeStruct((1, F), f32),
            jax.ShapeDtypeStruct((2, D), f32),
            jax.ShapeDtypeStruct((4, D), f32),
        ],
        in_specs=[spec] * 11,
        out_specs=[spec] * 10,
        scratch_shapes=scratch,
        compiler_params=pltpu.CompilerParams(
            collective_id=0, has_side_effects=True, vmem_limit_bytes=60 * 1024 * 1024
        ),
        name="layer",
    )(
        block_input[0],
        seg,
        wq,
        w_out.T,
        w_in,
        w_back.T,
        out_cotangent[0],
        qv_bias,
        in_bias[None],
        norm_gains,
        norm_biases,
    )
    block_out, input_grad, gq, go, gi, gb, gqv, ginb, ggain, gbias = outs
    return (block_out[None], input_grad[None], gq, go, gi, gb.T, gqv, ginb[0], ggain, gbias)


def solution(mesh):
    in_specs = (
        P("dp", "tensor", None),
        P("dp", "tensor"),
        P(None, "dp", "tensor"),
        P("tensor", "dp"),
        P("dp", "tensor"),
        P("tensor", "dp"),
        P(None, "tensor"),
        P("tensor"),
        P(),
        P(),
        P("dp", "tensor", None),
    )
    out_specs = (
        P("dp", "tensor", None),
        P("dp", "tensor", None),
        P(None, "dp", "tensor"),
        P("tensor", "dp"),
        P("dp", "tensor"),
        P("tensor", "dp"),
        P(None, "tensor"),
        P("tensor"),
        P(),
        P(),
    )
    nt, nd = mesh.shape["tensor"], mesh.shape["dp"]

    def body(*args):
        block_input, w_qkv, w_in = args[0], args[2], args[4]
        tokens, features = block_input.shape[1:]
        fits = (
            nd % 2 == 0
            and w_in.shape[0] % 16 == 0
            and tokens % 128 == 0
            and features % 128 == 0
            and w_in.shape[1] <= features
            and w_qkv.shape[2] % HEAD == 0
        )
        if fits:
            return kernel_shards(nt, nd, *args)
        return shards(*args)

    return jax.shard_map(body, mesh=mesh, in_specs=in_specs, out_specs=out_specs, check_vma=False)
```

```python
import functools
import math

import jax
import jax.numpy as jnp
from jax import lax
from jax.experimental import pallas as pl
from jax.experimental.pallas import tpu as pltpu
from jax.sharding import PartitionSpec as P

HEAD = 64


EPS = 1e-05
GELU_C = math.sqrt(2.0 / math.pi)
GELU_A = 0.044715


def normalize(residual, gain_row, offset_row):
    centered = residual - jnp.mean(residual, axis=-1, keepdims=True)
    inv_std = lax.rsqrt(jnp.mean(centered * centered, axis=-1, keepdims=True) + EPS)
    normed = centered * inv_std
    return (normed * gain_row + offset_row, normed, inv_std)


def normalize_back(upstream, normed, inv_std, gain_row):
    scaled = upstream * gain_row
    return inv_std * (
        scaled
        - jnp.mean(scaled, axis=-1, keepdims=True)
        - normed * jnp.mean(scaled * normed, axis=-1, keepdims=True)
    )


def gelu_pair(inputs):
    inner_arg = GELU_C * (inputs + GELU_A * inputs * inputs * inputs)
    tangent_h = jnp.tanh(inner_arg)
    value_out = 0.5 * inputs * (1.0 + tangent_h)
    slope_out = 0.5 * (1.0 + tangent_h) + 0.5 * inputs * (1.0 - tangent_h * tangent_h) * GELU_C * (
        1.0 + 3.0 * GELU_A * inputs * inputs
    )
    return (value_out, slope_out)


def contract_rows(left, right):
    return lax.dot_general(
        left, right, (((0,), (0,)), ((), ())), preferred_element_type=jnp.float32
    )


def contract_cols(left, right):
    return lax.dot_general(
        left, right, (((1,), (1,)), ((), ())), preferred_element_type=jnp.float32
    )


def masked_scores(query_block, key_rows, segment, key_end, num_heads):
    block_rows = query_block.shape[0]
    width = query_block.shape[1] // num_heads
    query_heads = query_block.reshape(block_rows, num_heads, width)
    key_heads = key_rows.reshape(key_end, num_heads, width)
    raw_scores = jnp.einsum(
        "qhd,khd->hqk", query_heads, key_heads, preferred_element_type=jnp.float32
    ) * (1.0 / math.sqrt(width))
    query_pos = jnp.arange(block_rows, dtype=jnp.int32)
    key_pos = jnp.arange(key_end, dtype=jnp.int32)
    allowed = (key_pos[None, :] <= query_pos[:, None]) & (segment[None, :] == segment[:, None])
    return jnp.where(allowed[None], raw_scores, -jnp.inf)


def attend_forward(queries, key_rows, values, segment, num_heads):
    total_rows = queries.shape[0]
    block_rows = min(512, total_rows)
    width = queries.shape[1] // num_heads
    scores = masked_scores(queries, key_rows, segment, block_rows, num_heads)
    row_max = jnp.max(scores, axis=-1, keepdims=True)
    log_total = row_max + jnp.log(jnp.sum(jnp.exp(scores - row_max), axis=-1, keepdims=True))
    weights = jnp.exp(scores - log_total).astype(jnp.bfloat16)
    value_heads = values.reshape(block_rows, num_heads, width)
    context = jnp.einsum("hqk,khd->qhd", weights, value_heads, preferred_element_type=jnp.float32)
    contexts = context.reshape(block_rows, num_heads * width).astype(jnp.bfloat16)
    return (contexts, log_total)


def attend_backward(
    queries, key_rows, values, segment, context, log_total, context_grad, num_heads
):
    total_rows = queries.shape[0]
    block_rows = min(512, total_rows)
    width = queries.shape[1] // num_heads
    inv_root = 1.0 / math.sqrt(width)
    key_grad = jnp.zeros((total_rows, num_heads, width), jnp.float32)
    value_grad = jnp.zeros((total_rows, num_heads, width), jnp.float32)
    scores = masked_scores(queries, key_rows, segment, block_rows, num_heads)
    probs = jnp.exp(scores - log_total)
    probs_half = probs.astype(jnp.bfloat16)
    grad_heads = context_grad.reshape(block_rows, num_heads, width)
    context_heads = context.reshape(block_rows, num_heads, width)
    value_heads = values.reshape(block_rows, num_heads, width)
    key_heads = key_rows.reshape(block_rows, num_heads, width)
    query_heads = queries.reshape(block_rows, num_heads, width)
    prob_grad = jnp.einsum(
        "qhd,khd->hqk", grad_heads, value_heads, preferred_element_type=jnp.float32
    )
    row_dot = jnp.transpose(
        jnp.sum(grad_heads.astype(jnp.float32) * context_heads.astype(jnp.float32), axis=-1)
    )[:, :, None]
    score_grad = (probs * (prob_grad - row_dot) * inv_root).astype(jnp.bfloat16)
    query_grads = jnp.einsum(
        "hqk,khd->qhd", score_grad, key_heads, preferred_element_type=jnp.float32
    ).reshape(block_rows, num_heads * width)
    key_grad = key_grad.at[:block_rows].add(
        jnp.einsum("hqk,qhd->khd", score_grad, query_heads, preferred_element_type=jnp.float32)
    )
    value_grad = value_grad.at[:block_rows].add(
        jnp.einsum("hqk,qhd->khd", probs_half, grad_heads, preferred_element_type=jnp.float32)
    )
    return (
        query_grads,
        key_grad.reshape(total_rows, num_heads * width),
        value_grad.reshape(total_rows, num_heads * width),
    )


def half_scatter(share):
    return lax.psum_scatter(
        share.astype(jnp.bfloat16), "tensor", scatter_dimension=0, tiled=True
    ).astype(jnp.float32)


def shards(
    block_input,
    segment_ids,
    w_qkv,
    w_out,
    w_in,
    w_back,
    qv_bias,
    in_bias,
    norm_gains,
    norm_biases,
    out_cotangent,
):
    bf16 = jnp.bfloat16
    residual = block_input[0].astype(jnp.float32)
    head_cols = w_qkv.shape[2]
    hidden_cols = w_in.shape[1]
    local_heads = head_cols // HEAD
    cuts = [head_cols, 2 * head_cols, 3 * head_cols, 4 * head_cols, 4 * head_cols + hidden_cols]
    packed = jnp.concatenate([w_qkv[0], w_qkv[1], w_qkv[2], w_out.T, w_in, w_back.T], axis=1)
    full = lax.all_gather(packed, "dp", axis=0, tiled=True)
    qkv_full = full[:, : cuts[2]]
    out_full = full[:, cuts[2] : cuts[3]]
    in_full = full[:, cuts[3] : cuts[4]]
    back_full = full[:, cuts[4] :]
    first_out, normed_first, inv_first = normalize(residual, norm_gains[0], norm_biases[0])
    first_half, segment, cotangent_full = (
        lax.all_gather(first_out.astype(bf16), "tensor", axis=0, tiled=True),
        lax.all_gather(segment_ids[0], "tensor", axis=0, tiled=True),
        lax.all_gather(out_cotangent[0], "tensor", axis=0, tiled=True),
    )
    projected = jnp.dot(first_half, qkv_full, preferred_element_type=jnp.float32)
    queries = (projected[:, : cuts[0]] + qv_bias[0]).astype(bf16)
    key_rows = projected[:, cuts[0] : cuts[1]].astype(bf16)
    values = (projected[:, cuts[1] :] + qv_bias[1]).astype(bf16)
    context, log_total = attend_forward(queries, key_rows, values, segment, local_heads)
    attn_share = half_scatter(contract_cols(context, out_full))
    middle = residual + attn_share + norm_biases[2]
    second_out, normed_second, inv_second = normalize(middle, norm_gains[1], norm_biases[1])
    second_half = lax.all_gather(second_out.astype(bf16), "tensor", axis=0, tiled=True)
    hidden_pre = jnp.dot(second_half, in_full, preferred_element_type=jnp.float32) + in_bias
    gelu_value, gelu_slope = gelu_pair(hidden_pre)
    activation = gelu_value.astype(bf16)
    mlp_share = half_scatter(contract_cols(activation, back_full))
    block_out = (middle + mlp_share + norm_biases[3]).astype(bf16)
    cotangent = out_cotangent[0].astype(jnp.float32)
    grad_back_part = contract_rows(cotangent_full, activation)
    hidden_grad = jnp.dot(cotangent_full, back_full, preferred_element_type=jnp.float32) * gelu_slope
    hidden_half = hidden_grad.astype(bf16)
    grad_in_part = contract_rows(second_half, hidden_half)
    second_grad = half_scatter(contract_cols(hidden_half, in_full))
    middle_grad = cotangent + normalize_back(second_grad, normed_second, inv_second, norm_gains[1])
    middle_full = lax.all_gather(middle_grad.astype(bf16), "tensor", axis=0, tiled=True)
    grad_out_part = contract_rows(middle_full, context)
    context_grad = jnp.dot(middle_full, out_full, preferred_element_type=jnp.float32).astype(bf16)
    query_grad, key_grad, value_grad = attend_backward(
        queries, key_rows, values, segment, context, log_total, context_grad, local_heads
    )
    proj_half = jnp.concatenate([query_grad, key_grad, value_grad], axis=1).astype(bf16)
    grad_qkv_part = contract_rows(first_half, proj_half)
    first_grad = half_scatter(contract_cols(proj_half, qkv_full))
    input_grad = middle_grad + normalize_back(first_grad, normed_first, inv_first, norm_gains[0])
    parts = jnp.concatenate(
        [grad_qkv_part, grad_out_part, grad_in_part, grad_back_part], axis=1
    ).astype(bf16)
    grads = lax.psum_scatter(parts, "dp", scatter_dimension=0, tiled=True).astype(jnp.float32)
    grad_qkv = jnp.stack([grads[:, : cuts[0]], grads[:, cuts[0] : cuts[1]], grads[:, cuts[1] : cuts[2]]])
    grad_out = grads[:, cuts[2] : cuts[3]].T
    grad_in = grads[:, cuts[3] : cuts[4]]
    grad_back = grads[:, cuts[4] :].T
    own = jnp.concatenate(
        [jnp.sum(query_grad, axis=0), jnp.sum(value_grad, axis=0), jnp.sum(hidden_grad, axis=0)]
    )
    tensors = lax.axis_size("tensor")
    rank = lax.axis_index("tensor")
    spread = jnp.where(jnp.arange(tensors)[:, None] == rank, own[None], 0.0)
    norm_terms = jnp.stack(
        [
            jnp.sum(first_grad * normed_first, axis=0),
            jnp.sum(second_grad * normed_second, axis=0),
            jnp.sum(first_grad, axis=0),
            jnp.sum(second_grad, axis=0),
            jnp.sum(middle_grad, axis=0),
            jnp.sum(cotangent, axis=0),
        ]
    )
    total = lax.psum(
        jnp.concatenate([spread.reshape(-1), norm_terms.reshape(-1)]), ("dp", "tensor")
    )
    width = own.shape[0]
    own_total = lax.dynamic_slice(total, (rank * width,), (width,))
    norm_total = total[tensors * width :].reshape(norm_terms.shape)
    return (
        block_out[None],
        input_grad[None],
        grad_qkv,
        grad_out,
        grad_in,
        grad_back,
        own_total[: 2 * head_cols].reshape(2, head_cols),
        own_total[2 * head_cols :],
        norm_total[:2],
        norm_total[2:],
    )


def matmul(left, right):
    return jnp.dot(left, right, preferred_element_type=jnp.float32)


def layer_kernel(
    nt,
    nd,
    x_ref,
    seg_ref,
    wq_ref,
    wo_ref,
    wi_ref,
    wb_ref,
    cot_ref,
    qvb_ref,
    inb_ref,
    gains_ref,
    biases_ref,
    bo_ref,
    ig_ref,
    gq_ref,
    go_ref,
    gi_ref,
    gb_ref,
    gqv_ref,
    ginb_ref,
    ggain_ref,
    gbias_ref,
    fq,
    fo,
    fi,
    fb,
    first_ref,
    second_ref,
    cot_full,
    mid_full,
    segs,
    qs,
    ks,
    vs,
    ctx,
    probs,
    hb,
    act,
    hh,
    cg,
    ph,
    send,
    recv,
    own,
    mid,
    norm1,
    norm2,
    mgrad,
    pq,
    po,
    pi,
    pb,
    aq,
    ao,
    ai,
    ab,
    bq,
    bo,
    bi,
    bb,
    rq,
    ro,
    ri,
    rb,
    small,
    zsmall,
    psmall,
    csmall,
    oq,
    oo,
    ob,
    zs,
    zr,
    ds,
    dr,
):
    bf16 = jnp.bfloat16
    f32 = jnp.float32
    nc = nd // 2
    t = lax.axis_index("tensor")
    d = lax.axis_index("dp")
    core = lax.rem(d, 2)
    chip = d // 2
    partner = chip * 2 + 1 - core
    T, D = x_ref.shape
    rows = wq_ref.shape[0]
    E = ctx.shape[1]
    heads = E // HEAD
    seq = nt * T
    weights = ((wq_ref, fq), (wo_ref, fo), (wi_ref, fi), (wb_ref, fb))
    grads = (
        (pq, aq, bq, rq, oq),
        (po, ao, bo, ro, oo),
        (pi, ai, bi, ri, gi_ref),
        (pb, ab, bb, rb, ob),
    )

    def remote(src, dst, ssem, rsem, **where):
        return pltpu.make_async_remote_copy(
            src_ref=src,
            dst_ref=dst,
            send_sem=ssem,
            recv_sem=rsem,
            device_id=where,
            device_id_type=pl.DeviceIdType.MESH,
        )

    def blk(index, size=T):
        return pl.ds(pl.multiple_of(index * size, size), size)

    def other(k):
        return lax.rem(t + k, nt)

    def chip_at(k):
        return lax.rem(chip + k, nc)

    def zcopy(kind, k, src, dst):
        return remote(src, dst, zs.at[kind, k], zr.at[kind, t], tensor=other(k))

    def zwait(kind, k, dst):
        remote(dst, dst, zs.at[kind, 0], zr.at[kind, other(k)], tensor=other(k)).wait_recv()

    sent = []

    def go_send(copy):
        copy.start()
        sent.append(copy)

    def line_copy(kind, slot, ref, b, to):
        piece = ref.at[blk(b)]
        return remote(piece, piece, zs.at[kind, slot], zr.at[kind, b], tensor=to)

    def line_own(kind, ref, act_on):
        for slot, to in ((0, t + 1), (2 * nt - 1, t - 1)):

            @pl.when((to >= 0) & (to < nt))
            def _():
                act_on(line_copy(kind, slot, ref, t, to))

    def line_place(s):
        sign = 2 * lax.rem(s, 2) - 1
        return t + sign * ((s + 1) // 2), t - sign

    def gather_send(kind, ref):
        line_own(kind, ref, lambda copy: copy.start())

    def gather_each(kind, ref, work):
        def step(s, carry):
            b, to = line_place(s)

            @pl.when((b >= 0) & (b < nt))
            def _():
                @pl.when(s > 0)
                def _():
                    remote(
                        ref.at[blk(b)], ref.at[blk(b)], zs.at[kind, 0], zr.at[kind, b], tensor=b
                    ).wait_recv()

                    @pl.when((to >= 0) & (to < nt))
                    def _():
                        line_copy(kind, s, ref, b, to).start()

                work(b, s)

            return carry

        lax.fori_loop(0, 2 * nt - 1, step, 0)

    def gather_drain(kind, ref):
        line_own(kind, ref, lambda copy: copy.wait_send())

        def step(s, carry):
            b, to = line_place(s)

            @pl.when((b >= 0) & (b < nt) & (to >= 0) & (to < nt))
            def _():
                line_copy(kind, s, ref, b, to).wait_send()

            return carry

        lax.fori_loop(1, 2 * nt - 1, step, 0)

    barrier = pltpu.get_barrier_semaphore()
    for k in range(1, nt):
        pl.semaphore_signal(
            barrier, inc=1, device_id={"tensor": other(k)}, device_id_type=pl.DeviceIdType.MESH
        )
    for k in range(1, nc):
        pl.semaphore_signal(
            barrier,
            inc=1,
            device_id={"dp": chip_at(k) * 2 + core},
            device_id_type=pl.DeviceIdType.MESH,
        )
    pl.semaphore_signal(
        barrier, inc=1, device_id={"dp": partner}, device_id_type=pl.DeviceIdType.MESH
    )
    pl.semaphore_wait(barrier, nt - 1 + nc - 1 + 1)

    def weight_send(w):
        src, full = weights[w]
        for k in range(1, nc):
            go_send(
                remote(
                    src,
                    full.at[blk(d, rows)],
                    ds.at[0, w, k],
                    dr.at[0, w, chip],
                    dp=chip_at(k) * 2 + core,
                )
            )
        go_send(
            remote(src, full.at[blk(d, rows)], ds.at[1, w, 0], dr.at[1, w, chip], dp=partner)
        )
        full[blk(d, rows), :] = src[...]

    def weight_pass(w):
        full = weights[w][1]
        for k in range(1, nc):
            c = chip_at(k)
            piece = full.at[blk(c * 2 + core, rows)]
            remote(piece, piece, ds.at[0, w, 0], dr.at[0, w, c], dp=c * 2 + core).wait_recv()
            go_send(remote(piece, piece, ds.at[1, w, k], dr.at[1, w, c], dp=partner))

    def weight_wait(w):
        full = weights[w][1]
        for k in range(nc):
            c = chip_at(k)
            piece = full.at[blk(c * 2 + 1 - core, rows)]
            remote(piece, piece, ds.at[1, w, 0], dr.at[1, w, c], dp=partner).wait_recv()

    weight_send(0)
    residual = x_ref[...].astype(f32)
    first_out, normed_first, inv_first = normalize(residual, gains_ref[0:1], biases_ref[0:1])
    norm1[...] = normed_first
    first_ref[blk(t), :] = first_out.astype(bf16)
    gather_send(0, first_ref)
    segs[t] = seg_ref[...]
    for k in range(1, nt):
        go_send(zcopy(1, k, seg_ref, segs.at[t]))
    for w in (1, 2, 3):
        weight_send(w)
    cot_full[blk(t), :] = cot_ref[...]
    for k in range(1, nt):
        go_send(zcopy(2, k, cot_ref, cot_full.at[blk(t)]))
    weight_pass(0)
    weight_wait(0)

    def project(b, s):
        out = matmul(first_ref[blk(b), :], fq[...])
        qs[blk(b), :] = (out[:, :E] + qvb_ref[0:1]).astype(bf16)
        ks[blk(b), :] = out[:, E : 2 * E].astype(bf16)
        vs[blk(b), :] = (out[:, 2 * E :] + qvb_ref[1:2]).astype(bf16)

    gather_each(0, first_ref, project)
    for k in range(1, nt):
        zwait(1, k, segs.at[other(k)])
    weight_pass(1)

    reach = (seq // 2 - 1 + T - 1) // T
    inv_root = 1.0 / math.sqrt(HEAD)
    for b in range(nt):
        low = max(0, b - reach)
        width = (b + 1 - low) * T
        key_seg = jnp.concatenate(
            [segs[j][0:1].astype(f32) for j in range(low, b + 1)], axis=1
        )
        query_seg = jnp.transpose(jnp.broadcast_to(segs[b][0:1].astype(f32), (T, T)))[:, 0:1]
        query_pos = lax.broadcasted_iota(jnp.int32, (T, width), 0) + b * T
        key_pos = lax.broadcasted_iota(jnp.int32, (T, width), 1) + low * T
        allowed = (key_pos <= query_pos) & (query_seg == key_seg)
        for h in range(heads):
            cols = slice(h * HEAD, (h + 1) * HEAD)
            scores = (
                contract_cols(qs[b * T : (b + 1) * T, cols], ks[low * T : (b + 1) * T, cols])
                * inv_root
            )
            scores = jnp.where(allowed, scores, -jnp.inf)
            row_max = jnp.max(scores, axis=-1, keepdims=True)
            log_total = row_max + jnp.log(
                jnp.sum(jnp.exp(scores - row_max), axis=-1, keepdims=True)
            )
            prob = jnp.exp(scores - log_total)
            probs[h, b, :, :width] = prob
            ctx[b * T : (b + 1) * T, cols] = matmul(
                prob.astype(bf16), vs[low * T : (b + 1) * T, cols]
            ).astype(bf16)
    weight_wait(1)

    def scatter(kind, slot, make):
        def step(s, carry):
            b = other(s + 1)
            share = make(b)

            @pl.when(s < nt - 1)
            def _():
                send[slot, b] = share.astype(bf16)
                zcopy(kind, s + 1, send.at[slot, b], recv.at[slot, t]).start()

            @pl.when(s == nt - 1)
            def _():
                own[slot] = share

            return carry

        lax.fori_loop(0, nt, step, 0)
        for k in range(1, nt):
            sent.append(zcopy(kind, k, send.at[slot, other(k)], recv.at[slot, t]))

    def scattered(kind, slot):
        total = own[slot]
        for k in range(1, nt):
            zwait(kind, k, recv.at[slot, other(k)])
            total = total + recv[slot, other(k)].astype(f32)
        return total

    scatter(5, 0, lambda b: contract_cols(ctx[blk(b), :], fo[...]))
    weight_pass(2)
    weight_pass(3)
    weight_wait(3)
    middle = residual + scattered(5, 0) + biases_ref[2:3]
    mid[...] = middle
    second_out, normed_second, inv_second = normalize(middle, gains_ref[1:2], biases_ref[1:2])
    norm2[...] = normed_second
    second_ref[blk(t), :] = second_out.astype(bf16)
    gather_send(3, second_ref)

    def back_step(s, carry):
        b = other(s)

        @pl.when(s > 0)
        def _():
            zwait(2, s, cot_full.at[blk(b)])

        hb[blk(b), :] = matmul(cot_full[blk(b), :], fb[...])
        return carry

    lax.fori_loop(0, nt, back_step, 0)
    weight_wait(2)
    small[...] = jnp.zeros_like(small)

    def hidden_step(b, s):
        pre = matmul(second_ref[blk(b), :], fi[...]) + inb_ref[...]
        value, slope = gelu_pair(pre)
        act[blk(b), :] = value.astype(bf16)
        grad = hb[blk(b), :] * slope
        small[8:9, : grad.shape[1]] += jnp.sum(grad, axis=0, keepdims=True)
        half = grad.astype(bf16)
        hh[blk(b), :] = half
        share = contract_cols(half, fi[...])

        @pl.when(s > 0)
        def _():
            send[1, b] = share.astype(bf16)
            zcopy(6, lax.rem(b - t + nt, nt), send.at[1, b], recv.at[1, t]).start()

        @pl.when(s == 0)
        def _():
            own[1] = share

    gather_each(3, second_ref, hidden_step)
    for k in range(1, nt):
        sent.append(zcopy(6, k, send.at[1, other(k)], recv.at[1, t]))

    def weight_grad(w, left, right):
        part, first_recv = grads[w][0], grads[w][1]
        step = 128

        def chunk(c, carry):
            part[blk(c, step), :] = contract_rows(left[:, blk(c, step)], right[...]).astype(bf16)
            return carry

        lax.fori_loop(0, D // step, chunk, 0)
        for c in range(nc):
            go_send(
                remote(
                    part.at[blk(c * 2 + 1 - core, rows)],
                    first_recv.at[c],
                    ds.at[2, w, c],
                    dr.at[2, w, c],
                    dp=partner,
                )
            )

    def pair_sum(w, c):
        part, first_recv = grads[w][0], grads[w][1]
        piece = first_recv.at[c]
        remote(piece, piece, ds.at[2, w, 0], dr.at[2, w, c], dp=partner).wait_recv()
        return part[blk(c * 2 + core, rows), :].astype(f32) + first_recv[c].astype(f32)

    def grad_pass(w):
        pairs, second_recv, out = grads[w][2], grads[w][3], grads[w][4]
        for k in range(1, nc):
            c = chip_at(k)
            pairs[c] = pair_sum(w, c).astype(bf16)
            go_send(
                remote(
                    pairs.at[c],
                    second_recv.at[chip],
                    ds.at[3, w, k],
                    dr.at[3, w, chip],
                    dp=c * 2 + core,
                )
            )
        out[...] = pair_sum(w, chip)

    def grad_finish(w):
        second_recv, out = grads[w][3], grads[w][4]
        total = out[...]
        for k in range(1, nc):
            c = chip_at(k)
            piece = second_recv.at[c]
            remote(piece, piece, ds.at[3, w, 0], dr.at[3, w, c], dp=c * 2 + core).wait_recv()
            total = total + second_recv[c].astype(f32)
        if w == 0:
            for c in range(3):
                gq_ref[c] = total[:, c * E : (c + 1) * E]
        elif w == 1:
            go_ref[...] = jnp.transpose(total)
        elif w == 2:
            gi_ref[...] = total
        else:
            gb_ref[...] = total

    weight_grad(2, second_ref, hh)
    second_grad = scattered(6, 1)
    cotangent = cot_ref[...].astype(f32)
    middle_grad = cotangent + normalize_back(second_grad, norm2[...], inv_second, gains_ref[1:2])
    mgrad[...] = middle_grad
    mid_full[blk(t), :] = middle_grad.astype(bf16)
    gather_send(4, mid_full)
    small[1:2, :] = jnp.sum(second_grad * norm2[...], axis=0, keepdims=True)
    small[3:4, :] = jnp.sum(second_grad, axis=0, keepdims=True)
    small[4:5, :] = jnp.sum(middle_grad, axis=0, keepdims=True)
    small[5:6, :] = jnp.sum(cotangent, axis=0, keepdims=True)
    weight_grad(3, cot_full, act)
    scatter(7, 2, lambda b: contract_cols(act[blk(b), :], fb[...]))
    grad_pass(2)
    grad_pass(3)

    def context_step(b, s):
        cg[blk(b), :] = matmul(mid_full[blk(b), :], fo[...]).astype(bf16)

    gather_each(4, mid_full, context_step)

    for h in range(heads):
        cols = slice(h * HEAD, (h + 1) * HEAD)
        key_grads = [None] * nt
        value_grads = [None] * nt
        query_sum = 0.0
        for b in range(nt):
            low = max(0, b - reach)
            width = (b + 1 - low) * T
            here, window = slice(b * T, (b + 1) * T), slice(low * T, (b + 1) * T)
            prob = probs[h, b, :, :width]
            grad = cg[here, cols]
            prob_grad = contract_cols(grad, vs[window, cols])
            row_dot = jnp.sum(
                grad.astype(f32) * ctx[here, cols].astype(f32), axis=-1, keepdims=True
            )
            score_grad = (prob * (prob_grad - row_dot) * inv_root).astype(bf16)
            query_grad = matmul(score_grad, ks[window, cols])
            query_sum = query_sum + jnp.sum(query_grad, axis=0, keepdims=True)
            ph[here, h * HEAD : (h + 1) * HEAD] = query_grad.astype(bf16)
            key_part = contract_rows(score_grad, qs[here, cols])
            value_part = contract_rows(prob.astype(bf16), grad)
            for j in range(low, b + 1):
                at = slice((j - low) * T, (j - low + 1) * T)
                fresh = key_grads[j] is None
                key_grads[j] = key_part[at] if fresh else key_grads[j] + key_part[at]
                value_grads[j] = value_part[at] if fresh else value_grads[j] + value_part[at]
        value_sum = 0.0
        for j in range(nt):
            here = slice(j * T, (j + 1) * T)
            ph[here, E + h * HEAD : E + (h + 1) * HEAD] = key_grads[j].astype(bf16)
            ph[here, 2 * E + h * HEAD : 2 * E + (h + 1) * HEAD] = value_grads[j].astype(bf16)
            value_sum = value_sum + jnp.sum(value_grads[j], axis=0, keepdims=True)
        small[9:10, h * HEAD : (h + 1) * HEAD] = query_sum
        small[10:11, h * HEAD : (h + 1) * HEAD] = value_sum

    scatter(8, 3, lambda b: contract_cols(ph[blk(b), :], fq[...]))
    weight_grad(0, first_ref, ph)
    weight_grad(1, mid_full, ctx)
    grad_pass(0)
    grad_pass(1)
    bo_ref[...] = (mid[...] + scattered(7, 2) + biases_ref[3:4]).astype(bf16)
    for w in (2, 3):
        grad_finish(w)
    first_grad = scattered(8, 3)
    ig_ref[...] = mgrad[...] + normalize_back(
        first_grad, norm1[...], inv_first, gains_ref[0:1]
    )
    small[0:1, :] = jnp.sum(first_grad * norm1[...], axis=0, keepdims=True)
    small[2:3, :] = jnp.sum(first_grad, axis=0, keepdims=True)
    zsmall[t] = small[0:8, :]
    for k in range(1, nt):
        go_send(zcopy(9, k, zsmall.at[t], zsmall.at[t]))
    for k in range(1, nt):
        zwait(9, k, zsmall.at[other(k)])
    summed = zsmall[0]
    for k in range(1, nt):
        summed = summed + zsmall[k]
    psmall[core] = jnp.concatenate([summed, small[8:16, :]], axis=0)
    go_send(
        remote(psmall.at[core], psmall.at[core], ds.at[2, 4, 0], dr.at[2, 4, 0], dp=partner)
    )
    piece = psmall.at[1 - core]
    remote(piece, piece, ds.at[2, 4, 1], dr.at[2, 4, 0], dp=partner).wait_recv()
    csmall[chip] = psmall[0] + psmall[1]
    for k in range(1, nc):
        go_send(
            remote(
                csmall.at[chip],
                csmall.at[chip],
                ds.at[3, 4, k],
                dr.at[3, 4, chip],
                dp=chip_at(k) * 2 + core,
            )
        )
    for w in (0, 1):
        grad_finish(w)
    for k in range(1, nc):
        c = chip_at(k)
        piece = csmall.at[c]
        remote(piece, piece, ds.at[3, 4, 0], dr.at[3, 4, c], dp=c * 2 + core).wait_recv()
    total = csmall[0]
    for c in range(1, nc):
        total = total + csmall[c]
    gqv_ref[...] = total[9:11, :E]
    ginb_ref[...] = total[8:9, : inb_ref.shape[1]]
    ggain_ref[...] = total[0:2]
    gbias_ref[...] = total[2:6]
    for kind, ref in ((0, first_ref), (3, second_ref), (4, mid_full)):
        gather_drain(kind, ref)
    for copy in sent:
        copy.wait_send()


def kernel_shards(
    nt,
    nd,
    block_input,
    segment_ids,
    w_qkv,
    w_out,
    w_in,
    w_back,
    qv_bias,
    in_bias,
    norm_gains,
    norm_biases,
    out_cotangent,
):
    bf16, f32 = jnp.bfloat16, jnp.float32
    T, D = block_input.shape[1:]
    E, F = w_qkv.shape[2], w_in.shape[1]
    rows = D // nd
    seq = nt * T
    heads = E // HEAD
    nc = nd // 2
    reach = (seq // 2 - 1 + T - 1) // T
    window = min(nt, reach + 1) * T
    widths = (3 * E, E, F, F)
    wq = jnp.concatenate([w_qkv[0], w_qkv[1], w_qkv[2]], axis=1)
    seg = jnp.broadcast_to(segment_ids, (8, T))
    vm = pltpu.VMEM
    scratch = (
        [vm((D, n), bf16) for n in widths]
        + [vm((seq, D), bf16)] * 4
        + [vm((nt, 8, T), jnp.int32)]
        + [vm((seq, E), bf16)] * 4
        + [vm((heads, nt, T, window), f32)]
        + [vm((seq, F), f32), vm((seq, F), bf16), vm((seq, F), bf16)]
        + [vm((seq, E), bf16), vm((seq, 3 * E), bf16)]
        + [vm((4, nt, T, D), bf16)] * 2
        + [vm((4, T, D), f32)]
        + [vm((T, D), f32)] * 4
        + [vm((D, n), bf16) for n in widths]
        + [vm((nc, rows, n), bf16) for n in widths] * 3
        + [vm((16, D), f32), vm((nt, 8, D), f32), vm((2, 16, D), f32), vm((nc, 16, D), f32)]
        + [vm((rows, n), f32) for n in (3 * E, E, F)]
        + [pltpu.SemaphoreType.DMA((10, 2 * nt))] * 2
        + [pltpu.SemaphoreType.DMA((4, 5, nc))] * 2
    )
    spec = pl.BlockSpec(memory_space=pltpu.VMEM)
    outs = pl.pallas_call(
        functools.partial(layer_kernel, nt, nd),
        out_shape=[
            jax.ShapeDtypeStruct((T, D), bf16),
            jax.ShapeDtypeStruct((T, D), f32),
            jax.ShapeDtypeStruct((3, rows, E), f32),
            jax.ShapeDtypeStruct((E, rows), f32),
            jax.ShapeDtypeStruct((rows, F), f32),
            jax.ShapeDtypeStruct((rows, F), f32),
            jax.ShapeDtypeStruct((2, E), f32),
            jax.ShapeDtypeStruct((1, F), f32),
            jax.ShapeDtypeStruct((2, D), f32),
            jax.ShapeDtypeStruct((4, D), f32),
        ],
        in_specs=[spec] * 11,
        out_specs=[spec] * 10,
        scratch_shapes=scratch,
        compiler_params=pltpu.CompilerParams(
            collective_id=0, has_side_effects=True, vmem_limit_bytes=60 * 1024 * 1024
        ),
        name="layer",
    )(
        block_input[0],
        seg,
        wq,
        w_out.T,
        w_in,
        w_back.T,
        out_cotangent[0],
        qv_bias,
        in_bias[None],
        norm_gains,
        norm_biases,
    )
    block_out, input_grad, gq, go, gi, gb, gqv, ginb, ggain, gbias = outs
    return (block_out[None], input_grad[None], gq, go, gi, gb.T, gqv, ginb[0], ggain, gbias)


def solution(mesh):
    in_specs = (
        P("dp", "tensor", None),
        P("dp", "tensor"),
        P(None, "dp", "tensor"),
        P("tensor", "dp"),
        P("dp", "tensor"),
        P("tensor", "dp"),
        P(None, "tensor"),
        P("tensor"),
        P(),
        P(),
        P("dp", "tensor", None),
    )
    out_specs = (
        P("dp", "tensor", None),
        P("dp", "tensor", None),
        P(None, "dp", "tensor"),
        P("tensor", "dp"),
        P("dp", "tensor"),
        P("tensor", "dp"),
        P(None, "tensor"),
        P("tensor"),
        P(),
        P(),
    )
    nt, nd = mesh.shape["tensor"], mesh.shape["dp"]

    def body(*args):
        block_input, w_qkv, w_in = args[0], args[2], args[4]
        tokens, features = block_input.shape[1:]
        fits = (
            nd % 2 == 0
            and w_in.shape[0] % 16 == 0
            and tokens % 128 == 0
            and features % 128 == 0
            and w_in.shape[1] <= features
            and w_qkv.shape[2] % HEAD == 0
        )
        if fits:
            return kernel_shards(nt, nd, *args)
        return shards(*args)

    return jax.shard_map(body, mesh=mesh, in_specs=in_specs, out_specs=out_specs, check_vma=False)
```
